32 devices in a mesh: pipe: 4 (over x, core), rep: 8 (over z, y).
Axes of the slice: x: 2, y: 2, z: 4, core: 2. Of those that a mesh axis runs over, the one named last changes fastest.
Arguments:
- activations: bfloat16 [4, 8, 1, 8, 32, 384], P('pipe', 'rep'), may hold values from -8 to 8, as said below
- preactivation: bfloat16 [4, 8, 1, 8, 32, 384], P('pipe', 'rep'), may hold values from -6 to 6
- upstream: bfloat16 [4, 8, 1, 8, 32, 384], P('pipe', 'rep'), may hold values from -12 to 12, as said below
- weights: bfloat16 [4, 3456, 384], P('pipe'), may hold values from -0.109375 to 0.109375
- master: float32 [4, 8, 165888], P('pipe', 'rep'), may hold values from -0.3125 to 0.3125
- momentum: float32 [4, 8, 165888], P('pipe', 'rep'), may hold values from -6 to 6
Outputs:
- passed_grad: bfloat16 [4, 8, 1, 8, 32, 384], P('pipe', 'rep')
- new_momentum: float32 [4, 8, 165888], P('pipe', 'rep')
- new_weights: float32 [4, 8, 165888], P('pipe', 'rep')
The draws below stay inside these ranges and needn't reach their ends.
Inputs may be any that keep to these rules, and one draw needn't show every extreme that they name: `activations`: Normal-like values; replicas of one section share part of their values. `upstream`: Normal-like values with a scale that differs from replica to replica; replicas of one section share part of their values.
All inputs are finite; a program needn't handle non-finite values.
Results may differ from the reference program's by a relative error of at most 0.0057.
Values may be sent and summed in bfloat16 or wider, within the bound.
A program may use at most 64 MiB of HBM per device.

```python
import jax
import jax.numpy as jnp
from jax import lax

C = 384
KTAPS = 9
HROWS = 8
WCOLS = 32
FRAMES = 1
PARAMS = 1327104
BLOCK = 165888
N_PIPE = 4
N_REP = 8


def draw_activations(key, part):
    full_shape = (N_PIPE, N_REP, FRAMES, HROWS, WCOLS, C)
    common = jax.random.normal(jax.random.fold_in(key, 101), (N_PIPE, 1, FRAMES, HROWS, WCOLS, C), jnp.float32)
    noise = jax.random.normal(jax.random.fold_in(key, 202), full_shape, jnp.float32)
    band = jnp.arange(C) * 16 // C
    shared_band = ((band < 8) & (band % 2 == 0)).astype(jnp.float32)
    common_weight = 0.15 + shared_band * (1.94 - 0.15)
    noise_weight = 0.989 + shared_band * (0.486 - 0.989)
    blended = common_weight * common + noise_weight * noise
    return jnp.clip(blended, -8.0, 8.0).astype(jnp.bfloat16)


def draw_upstream(key, part):
    full_shape = (N_PIPE, N_REP, FRAMES, HROWS, WCOLS, C)
    common = jax.random.normal(jax.random.fold_in(key, 404), (N_PIPE, 1, FRAMES, HROWS, WCOLS, C), jnp.float32)
    noise = jax.random.normal(jax.random.fold_in(key, 505), full_shape, jnp.float32)
    ramp = jnp.arange(N_REP).astype(jnp.float32) / max(N_REP - 1, 1)
    jitter = jax.random.uniform(jax.random.fold_in(key, 606), (N_PIPE, N_REP), jnp.float32, 0.8, 1.25)
    replica_scale = (jnp.exp(jnp.log(3.0) * ramp)[None, :] * jitter).reshape(N_PIPE, N_REP, 1, 1, 1, 1)
    blended = replica_scale * (0.85 * common + 0.5 * noise)
    return jnp.clip(blended, -12.0, 12.0).astype(jnp.bfloat16)


def level_of(own_key, shape, cuts, smallest, top_value):
    loudness, own = 1.0, jax.random.fold_in(own_key, 6)
    for dim, blocks in cuts:
        heights = jnp.exp(jax.random.uniform(jax.random.fold_in(own, dim), (blocks,), jnp.float32, smallest / len(cuts), top_value / len(cuts)))
        loudness = loudness * jnp.repeat(heights, shape[dim] // blocks).reshape([-1 if axis == dim else 1 for axis in range(len(shape))])
    return loudness


def centred(stream_key, shape, deviation, reach, cuts=(), dtype=jnp.bfloat16):
    entries = deviation * jax.random.normal(stream_key, shape, jnp.float32)
    if cuts:
        entries = entries * level_of(stream_key, shape, cuts, -0.22, 0.18)
    return jnp.clip(entries, -reach, reach).astype(dtype)


def setup_inputs(seed: int = 0) -> dict:
    streams_of = jax.random.split(jax.random.key(seed), 7)
    activations = draw_activations(jax.random.fold_in(streams_of[6], 71), 0)
    preactivation = centred(streams_of[1], (N_PIPE, N_REP, FRAMES, HROWS, WCOLS, C), 1.5, 6.0, ((0, 4), (1, 8)))
    upstream = draw_upstream(jax.random.fold_in(streams_of[6], 71), 0)
    weights = centred(streams_of[3], (N_PIPE, KTAPS * C, C), (KTAPS * C) ** -0.5, 0.109375, ((0, 4),))
    master = centred(streams_of[4], (N_PIPE, N_REP, BLOCK), C ** -0.5, 0.3125, ((0, 4), (1, 8)), jnp.float32)
    momentum = centred(streams_of[5], (N_PIPE, N_REP, BLOCK), 1.0, 6.0, ((0, 4), (1, 8)), jnp.float32)
    return {"activations": activations, "preactivation": preactivation, "upstream": upstream, "weights": weights, "master": master, "momentum": momentum}


EPS = 1e-6


def tile_patches(tile_data):
    frames, tile_rows, tile_cols, channels = tile_data.shape
    padded = jnp.pad(tile_data, ((0, 0), (1, 1), (1, 1), (0, 0)))
    pieces = [padded[:, row_off:row_off + tile_rows, col_off:col_off + tile_cols, :] for row_off in range(3) for col_off in range(3)]
    return jnp.concatenate(pieces, axis=-1).reshape(frames * tile_rows * tile_cols, 9 * channels)


def local_backward(tile_data, preact_tile, upstream_tile, kernel):
    frames, tile_rows, tile_cols, channels = tile_data.shape
    pre_float = preact_tile.astype(jnp.float32)
    sigmoid_val = jax.nn.sigmoid(pre_float)
    local_grad = (upstream_tile.astype(jnp.float32) * sigmoid_val * (1.0 + pre_float * (1.0 - sigmoid_val))).astype(jnp.bfloat16)
    flat_grad = local_grad.reshape(-1, channels)
    patches = tile_patches(tile_data)
    weight_grad = lax.dot_general(patches, flat_grad, (((0,), (0,)), ((), ())), preferred_element_type=jnp.float32).astype(jnp.bfloat16)
    spread = lax.dot_general(flat_grad, kernel, (((1,), (1,)), ((), ())), preferred_element_type=jnp.float32)
    spread = spread.reshape(frames, tile_rows, tile_cols, 9, channels)
    padded = jnp.pad(spread, ((0, 0), (1, 1), (1, 1), (0, 0), (0, 0)))
    summed = jnp.zeros((frames, tile_rows, tile_cols, channels), jnp.float32)
    for row_off in range(3):
        for col_off in range(3):
            summed = summed + padded[:, 2 - row_off:2 - row_off + tile_rows, 2 - col_off:2 - col_off + tile_cols, row_off * 3 + col_off, :]
    return weight_grad, summed.astype(jnp.bfloat16)


def adasum_pair(pair_rows):
    lower = pair_rows[0].astype(jnp.float32)
    upper = pair_rows[1].astype(jnp.float32)
    cross = jnp.sum(lower * upper)
    lower_sq = jnp.sum(lower * lower)
    upper_sq = jnp.sum(upper * upper)
    merged = (1.0 - cross / (2.0 * lower_sq + EPS)) * lower + (1.0 - cross / (2.0 * upper_sq + EPS)) * upper
    return merged.astype(jnp.bfloat16)


def section_step(inputs):
    tile_data, preact_tile, upstream_tile, kernel, master_shards, momentum_shards = inputs

    def replica_step(replica_inputs):
        return local_backward(replica_inputs[0], replica_inputs[1], replica_inputs[2], kernel)

    weight_grads, input_grads = lax.map(replica_step, (tile_data, preact_tile, upstream_tile))
    vectors = weight_grads.reshape(N_REP, PARAMS)
    remaining = N_REP
    while remaining > 1:
        vectors = lax.map(adasum_pair, vectors.reshape(remaining // 2, 2, PARAMS))
        remaining = remaining // 2
    combined = vectors.reshape(N_REP, BLOCK).astype(jnp.float32)
    updated_momentum = 0.9 * momentum_shards + 0.0625 * combined
    updated_weights = master_shards - 0.02 * updated_momentum
    return input_grads, updated_momentum, updated_weights


def reference(activations, preactivation, upstream, weights, master, momentum):
    input_grads, new_momentum, new_weights = lax.map(section_step, (activations, preactivation, upstream, weights, master, momentum))
    passed_grad = jnp.concatenate([input_grads[1:], jnp.zeros_like(input_grads[:1])], axis=0)
    return passed_grad, new_momentum, new_weights
```

```python
import functools

import jax
import jax.numpy as jnp
from jax import lax
from jax.experimental import pallas as pl
from jax.experimental.pallas import tpu as pltpu
from jax.sharding import PartitionSpec as P

EPS = 1e-06


def swapped(shard, axis, stride):
    return lax.ppermute(shard, axis, [(i, i ^ 1 << stride) for i in range(lax.axis_size(axis))])


def from_behind(shard, axis, by):
    count = lax.axis_size(axis)
    pairs = [(i, i + by) for i in range(count) if 0 <= i + by < count]
    return lax.ppermute(shard, axis, pairs)


def shifted_patches(tile_data, flipped):
    frames, tile_rows, tile_cols, channels = tile_data.shape
    padded = jnp.pad(tile_data, ((0, 0), (1, 1), (1, 1), (0, 0)))
    if flipped:
        offsets = [(2 - row_off, 2 - col_off) for row_off in range(3) for col_off in range(3)]
    else:
        offsets = [(row_off, col_off) for row_off in range(3) for col_off in range(3)]
    pieces = [
        padded[:, first : first + tile_rows, second : second + tile_cols, :]
        for first, second in offsets
    ]
    return jnp.concatenate(pieces, axis=-1).reshape(frames * tile_rows * tile_cols, 9 * channels)


def local_backward(tile_data, preact_tile, upstream_tile, kernel):
    frames, tile_rows, tile_cols, channels = tile_data.shape
    pre_float = preact_tile.astype(jnp.float32)
    sigmoid_val = jax.nn.sigmoid(pre_float)
    local_grad = (
        upstream_tile.astype(jnp.float32) * sigmoid_val * (1.0 + pre_float * (1.0 - sigmoid_val))
    ).astype(jnp.bfloat16)
    flat_grad = local_grad.reshape(-1, channels)
    patches = shifted_patches(tile_data, False)
    weight_grad = lax.dot_general(
        patches, flat_grad, (((0,), (0,)), ((), ())), preferred_element_type=jnp.float32
    ).astype(jnp.bfloat16)
    grad_patches = shifted_patches(local_grad, True).reshape(-1, 9, channels)
    kernel_taps = kernel.reshape(9, channels, channels)
    summed = lax.dot_general(
        grad_patches, kernel_taps, (((1, 2), (0, 2)), ((), ())), preferred_element_type=jnp.float32
    )
    return (
        weight_grad,
        summed.astype(jnp.bfloat16).reshape(frames, tile_rows, tile_cols, channels),
    )


def group_sum(partials, sum_bits):
    for bit_number in range(sum_bits):
        partials = partials + swapped(partials, "rep", bit_number)
    return partials


def body(activations, preactivation, upstream, weights, master, momentum):
    weight_grad, input_grad = local_backward(
        activations[0, 0], preactivation[0, 0], upstream[0, 0], weights[0]
    )
    passed = from_behind(input_grad, "pipe", -1)
    replicas = lax.axis_size("rep")
    level_count = replicas.bit_length() - 1
    rep_index = lax.axis_index("rep")
    held_rows = weight_grad.reshape(replicas, -1)
    for level_num in range(level_count):
        is_lower = jnp.right_shift(rep_index, level_num) & 1 == 0
        paired = held_rows.reshape(-1, 2, held_rows.shape[1])
        keep_rows = jnp.where(is_lower, paired[:, 0], paired[:, 1])
        give_rows = jnp.where(is_lower, paired[:, 1], paired[:, 0])
        other_rows = swapped(give_rows, "rep", level_num)
        keep_float = keep_rows.astype(jnp.float32)
        other_float = other_rows.astype(jnp.float32)
        keep_sq = jnp.sum(keep_float * keep_float)
        other_sq = jnp.sum(other_float * other_float)
        partials = jnp.stack(
            [
                jnp.where(is_lower, keep_sq, other_sq),
                jnp.where(is_lower, other_sq, keep_sq),
                jnp.sum(keep_float * other_float),
            ]
        )
        sum_bits = level_num + 1
        partials = group_sum(partials, sum_bits)
        lower_coef = 1.0 - partials[2] / (2.0 * partials[0] + EPS)
        upper_coef = 1.0 - partials[2] / (2.0 * partials[1] + EPS)
        keep_coef = jnp.where(is_lower, lower_coef, upper_coef)
        other_coef = jnp.where(is_lower, upper_coef, lower_coef)
        merged = keep_coef * keep_rows.astype(jnp.float32) + other_coef * other_rows.astype(
            jnp.float32
        )
        held_rows = merged.astype(jnp.bfloat16)
    combined = held_rows.astype(jnp.float32).reshape(momentum.shape)
    new_momentum = 0.9 * momentum + 0.0625 * combined
    new_weights = master - 0.02 * new_momentum
    return (passed[None, None], new_momentum, new_weights)


MESH = pl.DeviceIdType.MESH
F32 = jnp.float32
BF16 = jnp.bfloat16


def fold(product):
    return jnp.sum(product.reshape(-1, 8, product.shape[-1]), axis=0)


def roles(z, y, rep):
    half = z // 2
    near = z + 1 - 2 * (z % 2)
    across = 2 - half
    far = 3 - 3 * half
    return half, near, across, far


def adasum_weights(gram):
    count = gram.shape[0]
    row = lax.broadcasted_iota(jnp.int32, gram.shape, 0)
    lane = lax.broadcasted_iota(jnp.int32, gram.shape, 1)
    weight = None
    bit = 1
    while bit < count:
        own = jnp.where(lane == row, gram, 0.0)
        cross = jnp.where(lane == row ^ bit, gram, 0.0)

        def coef(axis):
            sq = jnp.maximum(jnp.sum(own, axis=axis, keepdims=True), 0.0)
            return 1.0 - jnp.sum(cross, axis=axis, keepdims=True) / (2.0 * sq + EPS)

        down = coef(1)
        weight = down if weight is None else weight * down
        if 2 * bit < count:
            gram = down * gram * coef(0)
            gram = gram + jnp.where(
                row & bit == 0, pltpu.roll(gram, count - bit, 0), pltpu.roll(gram, bit, 0)
            )
            lanes = gram.shape[1]
            gram = gram + jnp.where(
                lane & bit == 0, pltpu.roll(gram, lanes - bit, 1), pltpu.roll(gram, bit, 1)
            )
        bit *= 2
    return weight


def kernel(
    sections, replicas, cols,
    act_hbm, pre_hbm, up_hbm, weights_hbm,
    passed_ref, combined_ref,
    act_v, pre_v, up_v, kernel_v, act_t, grad_v, grad_tiles,
    act_in, grad_in, patches, blocks, pair_sums, gram_in, merged, merged_in, shifted, igrad,
    load_sem, act_send, act_recv, grad_send, grad_recv, gram_send, gram_recv,
    merged_send, merged_recv, pass_sem,
):
    pixels, channels = act_v.shape
    part = channels // 4
    lanes = 128
    unit = channels // replicas
    pipe, rep = lax.axis_index("pipe"), lax.axis_index("rep")
    z, y = rep // 2, rep % 2
    half, near, across, far = roles(z, y, rep)
    outer = (z == 0) | (z == 3)
    inner = (z == 1) | (z == 2)
    quarter = half * 2 + y

    barrier = pltpu.get_barrier_semaphore()
    for step in range(1, replicas):
        peer = lax.rem(rep + step, replicas)
        pl.semaphore_signal(barrier, inc=1, device_id=(pipe, peer), device_id_type=MESH)

    @pl.when(pipe < sections - 1)
    def _():
        pl.semaphore_signal(barrier, inc=1, device_id=(pipe + 1, rep), device_id_type=MESH)

    loads = [
        pltpu.make_async_copy(src, dst, load_sem.at[n])
        for n, (src, dst) in enumerate(
            ((act_hbm, act_v), (pre_hbm, pre_v), (up_hbm, up_v), (weights_hbm, kernel_v))
        )
    ]
    for load in loads:
        load.start()

    def index(zz, yy):
        return zz * 2 + yy

    def remote(src, dst, send, recv, target):
        return pltpu.make_async_remote_copy(
            src_ref=src, dst_ref=dst, send_sem=send, recv_sem=recv,
            device_id=(pipe, target), device_id_type=MESH,
        )

    def act_own(slot, block_of, target):
        rows = pl.ds(pl.multiple_of(block_of * part, part), part)
        return remote(act_t.at[rows, :], act_in.at[rep], act_send.at[slot], act_recv.at[rep], target)

    def act_pass(slot, block):
        return remote(
            act_in.at[block], act_in.at[block], act_send.at[slot], act_recv.at[block], index(near, y)
        )

    def grad_copy(slot, i, src, block, target):
        return remote(
            src, grad_in.at[block, i], grad_send.at[slot, i], grad_recv.at[block, i], target
        )

    other_inner = 2 - half
    own_acts = (
        (0, quarter, index(near, y)),
        (1, half * 2 + 1 - y, index(z, 1 - y)),
        (2, (1 - half) * 2 + y, index(other_inner, y)),
        (3, (1 - half) * 2 + 1 - y, index(other_inner, 1 - y)),
    )
    order = [
        index(z, y), index(z, 1 - y), index(near, y), index(across, y),
        index(near, 1 - y), index(across, 1 - y), index(far, y), index(far, 1 - y),
    ]

    sent = []

    def start(cond, copies):
        if cond is None:
            for copy in copies:
                copy().start()
        else:
            @pl.when(cond)
            def _():
                for copy in copies:
                    copy().start()
        sent.append((cond, copies))

    def wait_act(block):
        act_pass(4, block).wait_recv()

    def wait_grad(block):
        grad_copy(0, 0, grad_in.at[block, 0], block, rep).wait_recv()

        @pl.when(inner)
        def _():
            grad_copy(0, 1, grad_in.at[block, 1], block, rep).wait_recv()

    def own_grad(slot, tiles, target):
        return [
            functools.partial(grad_copy, slot, i, grad_tiles.at[tile], rep, target)
            for i, tile in enumerate(tiles)
        ]

    def pass_grad(slot, block, target, extra=None):
        start(None, [functools.partial(grad_copy, slot, 0, grad_in.at[block, 0], block, target)])
        start(inner, [functools.partial(grad_copy, slot, 1, grad_in.at[block, 1], block, target)])

    def patch(block):
        tile = act_in[block].astype(F32)
        pixel = lax.broadcasted_iota(jnp.int32, (1, pixels), 1)
        column = pixel % cols
        for j in range(3):
            if j == 1:
                moved = tile
            else:
                moved = pltpu.roll(tile, (1 - j) % pixels, 1)
                moved = jnp.where(column > 0 if j == 0 else column < cols - 1, moved, 0.0)
            for i in range(3):
                if i == 1:
                    placed = moved
                else:
                    placed = pltpu.roll(moved, ((1 - i) * cols) % pixels, 1)
                    placed = jnp.where(
                        pixel >= cols if i == 0 else pixel < pixels - cols, placed, 0.0
                    )
                patches[block, pl.ds((i * 3 + j) * part, part), :] = placed.astype(BF16)

    def multiply(k):
        block = order[k]
        grad = jnp.concatenate([grad_in[block, 0], grad_in[block, 1]], axis=1)

        def step(t, sums):
            here = pl.ds(pl.multiple_of(t * part, part), part)
            new = jnp.dot(patches[block, here, :], grad, preferred_element_type=F32)
            blocks[block, here, :] = new
            out = []
            for m in range(k + 1):
                against = new if m == k else blocks[order[m], here, :]
                folded = fold(new * against)
                out.append(sums[m] + folded[:, :lanes] + folded[:, lanes:])
            return tuple(out)

        zero = jnp.zeros((8, lanes), F32)
        sums = lax.fori_loop(0, 9, step, (zero,) * (k + 1), unroll=3)
        for m in range(k + 1):
            total = jnp.sum(sums[m], axis=0, keepdims=True)
            pair_sums[order[m], pl.ds(block, 1), :] = total
            if m < k:
                pair_sums[block, pl.ds(order[m], 1), :] = total

    loads[0].wait()
    act_t[...] = act_v[...].T
    pl.semaphore_wait(barrier, replicas - 1 + (pipe > 0).astype(jnp.int32))
    start(None, [functools.partial(act_own, *args) for args in own_acts])
    loads[1].wait()
    loads[2].wait()
    z_f = pre_v[...].astype(F32)
    sig = jax.nn.sigmoid(z_f)
    grad = (up_v[...].astype(F32) * sig * (1.0 + z_f * (1.0 - sig))).astype(BF16)
    grad_v[...] = grad
    for tile in range(3):
        grad_tiles[tile] = grad[:, tile * lanes : (tile + 1) * lanes]
    start(inner, own_grad(1, (1, 2), index(across, y)))
    start(outer, own_grad(1, (1, 2), index(near, y)))
    start(inner, own_grad(0, (1, 2), index(z, 1 - y)))
    start(outer, own_grad(0, (0,), index(z, 1 - y)))
    start(outer, own_grad(2, (0,), index(far, y)))
    start(inner, own_grad(2, (0,), index(near, y)))
    start(inner, own_grad(3, (0,), index(far, y)))

    act_in[rep] = act_t[pl.ds(pl.multiple_of(quarter * part, part), part), :]

    @pl.when(outer)
    def _():
        grad_in[rep, 0] = grad_tiles[0]
        for block in range(replicas):
            grad_in[block, 1] = jnp.zeros((pixels, lanes), BF16)

    @pl.when(inner)
    def _():
        grad_in[rep, 0] = grad_tiles[1]
        grad_in[rep, 1] = grad_tiles[2]

    def relay(slot, k):
        @pl.when(inner)
        def _():
            wait_act(order[k])

        start(inner, [functools.partial(act_pass, slot, order[k])])

    def take(k, relayed):
        if relayed:
            @pl.when(outer)
            def _():
                wait_act(order[k])
        else:
            wait_act(order[k])
        patch(order[k])

    patch(rep)
    multiply(0)
    wait_act(order[1])
    start(None, [functools.partial(act_pass, 4, order[1])])
    relay(5, 3)
    relay(6, 5)
    patch(order[1])
    wait_grad(order[2])
    pass_grad(4, order[2], index(z, 1 - y))
    start(inner, [
        functools.partial(grad_copy, 5, i, grad_in.at[order[2], i], order[2], index(across, y))
        for i in range(2)
    ])
    relay(7, 6)
    relay(8, 7)
    wait_grad(order[1])
    multiply(1)
    wait_grad(order[3])
    pass_grad(6, order[3], index(z, 1 - y))
    take(2, False)
    multiply(2)
    take(3, True)
    multiply(3)
    take(4, False)
    take(5, True)
    wait_grad(order[4])
    multiply(4)
    wait_grad(order[6])
    pass_grad(7, order[6], index(z, 1 - y))
    wait_grad(order[5])
    multiply(5)
    take(6, True)
    multiply(6)
    take(7, True)
    wait_grad(order[7])
    multiply(7)

    lane = lax.broadcasted_iota(jnp.int32, (replicas, lanes), 1)
    gram = jnp.zeros((replicas, lanes), F32)
    for block in range(replicas):
        gram = jnp.where(lane == block, jnp.sum(pair_sums[block], axis=1, keepdims=True), gram)
    gram_in[rep] = gram

    def gram_copy(step):
        peer = lax.rem(rep + step, replicas)
        return remote(gram_in.at[rep], gram_in.at[rep], gram_send.at[step], gram_recv.at[rep], peer)

    def gram_from(step):
        peer = lax.rem(rep + step, replicas)
        return remote(gram_in.at[peer], gram_in.at[peer], gram_send.at[step], gram_recv.at[peer], peer)

    for step in range(1, replicas):
        start(None, [functools.partial(gram_copy, step)])

    edge = jnp.zeros((cols, channels), BF16)
    for j in range(3):
        shifted[j, pl.ds(0, cols), :] = edge
        shifted[j, pl.ds(cols + pixels, cols), :] = edge
    grad = grad_v[...].astype(F32)
    column = lax.broadcasted_iota(jnp.int32, (pixels, channels), 0) % cols
    here = pl.ds(cols, pixels)
    shifted[0, here, :] = jnp.where(column < cols - 1, pltpu.roll(grad, pixels - 1, 0), 0.0).astype(BF16)
    shifted[1, here, :] = grad_v[...]
    shifted[2, here, :] = jnp.where(column > 0, pltpu.roll(grad, 1, 0), 0.0).astype(BF16)
    loads[3].wait()
    total = jnp.zeros((pixels, channels), F32)
    for i in range(3):
        for j in range(3):
            total = total + lax.dot_general(
                shifted[j, pl.ds((2 - i) * cols, pixels), :],
                kernel_v[pl.ds((i * 3 + j) * channels, channels), :],
                (((1,), (1,)), ((), ())),
                preferred_element_type=F32,
            )
    igrad[...] = total.astype(BF16)

    @pl.when(pipe == sections - 1)
    def _():
        passed_ref[...] = jnp.zeros_like(passed_ref)

    passing = pltpu.make_async_remote_copy(
        src_ref=igrad,
        dst_ref=passed_ref,
        send_sem=pass_sem.at[0],
        recv_sem=pass_sem.at[1],
        device_id=(jnp.maximum(pipe - 1, 0), rep),
        device_id_type=MESH,
    )

    @pl.when(pipe > 0)
    def _():
        passing.start()

    for step in range(1, replicas):
        gram_from(step).wait_recv()
    gram = gram_in[0]
    for block in range(1, replicas):
        gram = gram + gram_in[block]
    weight = adasum_weights(gram)

    def merged_copy(t, cb, wide, owner, local):
        src = merged.at[t, cb] if wide else merged.at[t, cb, pl.ds(0, 1)]
        dst = merged_in.at[local, pl.ds(1, 2)] if wide else merged_in.at[local, pl.ds(0, 1)]
        kind = 1 if wide else 0
        return remote(src, dst, merged_send.at[t, cb], merged_recv.at[local, kind], owner)

    for t in range(9):
        tap = t + (1 - half) * (8 - 2 * t)
        here = pl.ds(pl.multiple_of(tap * part, part), part)
        total = weight[0:1, 0:1] * blocks[0, here, :]
        for block in range(1, replicas):
            total = total + weight[block : block + 1, 0:1] * blocks[block, here, :]
        total = total.astype(BF16)
        for cb in range(2):
            rows = slice(cb * unit, (cb + 1) * unit)
            merged[t, cb, 0] = total[rows, :lanes]
            merged[t, cb, 1] = total[rows, lanes:]
            place = tap * replicas + quarter * 2 + cb
            owner, local = place // 9, place % 9
            mine = owner == rep

            @pl.when(mine & outer)
            def _():
                merged_in[local, 0] = merged[t, cb, 0]

            @pl.when(mine & inner)
            def _():
                merged_in[local, 1] = merged[t, cb, 0]
                merged_in[local, 2] = merged[t, cb, 1]

            away = owner != rep
            start(away & outer, [functools.partial(merged_copy, t, cb, False, owner, local)])
            start(away & inner, [functools.partial(merged_copy, t, cb, True, owner, local)])

    for local in range(9):
        place = rep * 9 + local
        of = (place % replicas) // 2
        its_half, its_y = of // 2, of % 2
        for wide, plane in ((False, 3 * its_half), (True, 1 + its_half)):
            @pl.when(index(plane, its_y) != rep)
            def _():
                merged_copy(0, 0, wide, rep, local).wait_recv()
        for tile in range(3):
            at = pl.ds(local * unit * 3 + tile, unit, stride=3)
            combined_ref[at, :] = merged_in[local, tile].astype(F32)

    for cond, copies in sent:
        if cond is None:
            for copy in copies:
                copy().wait_send()
        else:
            @pl.when(cond)
            def _():
                for copy in copies:
                    copy().wait_send()

    @pl.when(pipe > 0)
    def _():
        passing.wait_send()

    @pl.when(pipe < sections - 1)
    def _():
        passing.wait_recv()


def factor_body(sections, replicas, activations, preactivation, upstream, weights, master, momentum):
    tile = activations.shape[3:]
    cols, channels = tile[1], tile[2]
    pixels = tile[0] * cols
    taps_rows = weights.shape[1]
    lanes = 128
    part, unit = channels // 4, channels // replicas
    flat = (momentum.shape[2] // lanes, lanes)
    small, big = pl.BlockSpec(memory_space=pltpu.VMEM), pl.BlockSpec(memory_space=pl.ANY)
    passed, combined = pl.pallas_call(
        functools.partial(kernel, sections, replicas, cols),
        out_shape=(
            jax.ShapeDtypeStruct((pixels, channels), BF16),
            jax.ShapeDtypeStruct(flat, F32),
        ),
        in_specs=[big] * 4,
        out_specs=(small, small),
        scratch_shapes=[
            pltpu.VMEM((pixels, channels), BF16),
            pltpu.VMEM((pixels, channels), BF16),
            pltpu.VMEM((pixels, channels), BF16),
            pltpu.VMEM((taps_rows, channels), BF16),
            pltpu.VMEM((channels, pixels), BF16),
            pltpu.VMEM((pixels, channels), BF16),
            pltpu.VMEM((3, pixels, lanes), BF16),
            pltpu.VMEM((replicas, part, pixels), BF16),
            pltpu.VMEM((replicas, 2, pixels, lanes), BF16),
            pltpu.VMEM((replicas, 9 * part, pixels), BF16),
            pltpu.VMEM((replicas, 9 * part, 2 * lanes), F32),
            pltpu.VMEM((replicas, replicas, lanes), F32),
            pltpu.VMEM((replicas, replicas, lanes), F32),
            pltpu.VMEM((9, 2, 2, unit, lanes), BF16),
            pltpu.VMEM((9, 3, unit, lanes), BF16),
            pltpu.VMEM((3, pixels + 2 * cols, channels), BF16),
            pltpu.VMEM((pixels, channels), BF16),
            pltpu.SemaphoreType.DMA((4,)),
            pltpu.SemaphoreType.DMA((9,)),
            pltpu.SemaphoreType.DMA((replicas,)),
            pltpu.SemaphoreType.DMA((8, 2)),
            pltpu.SemaphoreType.DMA((replicas, 2)),
            pltpu.SemaphoreType.DMA((replicas,)),
            pltpu.SemaphoreType.DMA((replicas,)),
            pltpu.SemaphoreType.DMA((9, 2)),
            pltpu.SemaphoreType.DMA((9, 2)),
            pltpu.SemaphoreType.DMA((2,)),
        ],
        compiler_params=pltpu.CompilerParams(
            collective_id=0, has_side_effects=True, vmem_limit_bytes=40 * 1024 * 1024
        ),
    )(
        activations.reshape(pixels, channels),
        preactivation.reshape(pixels, channels),
        upstream.reshape(pixels, channels),
        weights[0],
    )
    combined = combined.reshape(momentum.shape)
    new_momentum = 0.9 * momentum + 0.0625 * combined
    new_weights = master - 0.02 * new_momentum
    return passed.reshape(activations.shape), new_momentum, new_weights


def pick(sections, replicas, *arrays):
    activations, weights, momentum = arrays[0], arrays[3], arrays[5]
    channels = activations.shape[5]
    fits = (
        replicas == 8
        and activations.shape[2] == 1
        and weights.shape[1] == 9 * channels
        and weights.shape[2] == channels
        and channels == 3 * 128
        and (activations.shape[3] * activations.shape[4]) % 128 == 0
        and activations.shape[4] % 16 == 0
        and momentum.shape[2] % 1024 == 0
    )
    return factor_body(sections, replicas, *arrays) if fits else body(*arrays)


def solution(mesh):
    return jax.shard_map(
        functools.partial(pick, mesh.shape["pipe"], mesh.shape["rep"]),
        mesh=mesh,
        in_specs=(
            P("pipe", "rep", None, None, None, None),
            P("pipe", "rep", None, None, None, None),
            P("pipe", "rep", None, None, None, None),
            P("pipe", None, None),
            P("pipe", "rep", None),
            P("pipe", "rep", None),
        ),
        out_specs=(
            P("pipe", "rep", None, None, None, None),
            P("pipe", "rep", None),
            P("pipe", "rep", None),
        ),
        check_vma=False,
    )
```

```python
import functools

import jax
import jax.numpy as jnp
from jax import lax
from jax.experimental import pallas as pl
from jax.experimental.pallas import tpu as pltpu
from jax.sharding import PartitionSpec as P

EPS = 1e-06


def swapped(shard, axis, stride):
    return lax.ppermute(shard, axis, [(i, i ^ 1 << stride) for i in range(lax.axis_size(axis))])


def from_behind(shard, axis, by):
    count = lax.axis_size(axis)
    pairs = [(i, i + by) for i in range(count) if 0 <= i + by < count]
    return lax.ppermute(shard, axis, pairs)


def shifted_patches(tile_data, flipped):
    frames, tile_rows, tile_cols, channels = tile_data.shape
    padded = jnp.pad(tile_data, ((0, 0), (1, 1), (1, 1), (0, 0)))
    if flipped:
        offsets = [(2 - row_off, 2 - col_off) for row_off in range(3) for col_off in range(3)]
    else:
        offsets = [(row_off, col_off) for row_off in range(3) for col_off in range(3)]
    pieces = [
        padded[:, first : first + tile_rows, second : second + tile_cols, :]
        for first, second in offsets
    ]
    return jnp.concatenate(pieces, axis=-1).reshape(frames * tile_rows * tile_cols, 9 * channels)


def local_backward(tile_data, preact_tile, upstream_tile, kernel):
    frames, tile_rows, tile_cols, channels = tile_data.shape
    pre_float = preact_tile.astype(jnp.float32)
    sigmoid_val = jax.nn.sigmoid(pre_float)
    local_grad = (
        upstream_tile.astype(jnp.float32) * sigmoid_val * (1.0 + pre_float * (1.0 - sigmoid_val))
    ).astype(jnp.bfloat16)
    flat_grad = local_grad.reshape(-1, channels)
    patches = shifted_patches(tile_data, False)
    weight_grad = lax.dot_general(
        patches, flat_grad, (((0,), (0,)), ((), ())), preferred_element_type=jnp.float32
    ).astype(jnp.bfloat16)
    grad_patches = shifted_patches(local_grad, True).reshape(-1, 9, channels)
    kernel_taps = kernel.reshape(9, channels, channels)
    summed = lax.dot_general(
        grad_patches, kernel_taps, (((1, 2), (0, 2)), ((), ())), preferred_element_type=jnp.float32
    )
    return (
        weight_grad,
        summed.astype(jnp.bfloat16).reshape(frames, tile_rows, tile_cols, channels),
    )


def group_sum(partials, sum_bits):
    for bit_number in range(sum_bits):
        partials = partials + swapped(partials, "rep", bit_number)
    return partials


def body(activations, preactivation, upstream, weights, master, momentum):
    weight_grad, input_grad = local_backward(
        activations[0, 0], preactivation[0, 0], upstream[0, 0], weights[0]
    )
    passed = from_behind(input_grad, "pipe", -1)
    replicas = lax.axis_size("rep")
    level_count = replicas.bit_length() - 1
    rep_index = lax.axis_index("rep")
    held_rows = weight_grad.reshape(replicas, -1)
    for level_num in range(level_count):
        is_lower = jnp.right_shift(rep_index, level_num) & 1 == 0
        paired = held_rows.reshape(-1, 2, held_rows.shape[1])
        keep_rows = jnp.where(is_lower, paired[:, 0], paired[:, 1])
        give_rows = jnp.where(is_lower, paired[:, 1], paired[:, 0])
        other_rows = swapped(give_rows, "rep", level_num)
        keep_float = keep_rows.astype(jnp.float32)
        other_float = other_rows.astype(jnp.float32)
        keep_sq = jnp.sum(keep_float * keep_float)
        other_sq = jnp.sum(other_float * other_float)
        partials = jnp.stack(
            [
                jnp.where(is_lower, keep_sq, other_sq),
                jnp.where(is_lower, other_sq, keep_sq),
                jnp.sum(keep_float * other_float),
            ]
        )
        sum_bits = level_num + 1
        partials = group_sum(partials, sum_bits)
        lower_coef = 1.0 - partials[2] / (2.0 * partials[0] + EPS)
        upper_coef = 1.0 - partials[2] / (2.0 * partials[1] + EPS)
        keep_coef = jnp.where(is_lower, lower_coef, upper_coef)
        other_coef = jnp.where(is_lower, upper_coef, lower_coef)
        merged = keep_coef * keep_rows.astype(jnp.float32) + other_coef * other_rows.astype(
            jnp.float32
        )
        held_rows = merged.astype(jnp.bfloat16)
    combined = held_rows.astype(jnp.float32).reshape(momentum.shape)
    new_momentum = 0.9 * momentum + 0.0625 * combined
    new_weights = master - 0.02 * new_momentum
    return (passed[None, None], new_momentum, new_weights)


MESH = pl.DeviceIdType.MESH
F32 = jnp.float32
BF16 = jnp.bfloat16


def fold(product):
    return jnp.sum(product.reshape(-1, 8, product.shape[-1]), axis=0)


def roles(z, y, rep):
    half = z // 2
    near = z + 1 - 2 * (z % 2)
    across = 2 - half
    far = 3 - 3 * half
    return half, near, across, far


def adasum_weights(gram):
    count = gram.shape[0]
    row = lax.broadcasted_iota(jnp.int32, gram.shape, 0)
    lane = lax.broadcasted_iota(jnp.int32, gram.shape, 1)
    weight = None
    bit = 1
    while bit < count:
        own = jnp.where(lane == row, gram, 0.0)
        cross = jnp.where(lane == row ^ bit, gram, 0.0)

        def coef(axis):
            sq = jnp.maximum(jnp.sum(own, axis=axis, keepdims=True), 0.0)
            return 1.0 - jnp.sum(cross, axis=axis, keepdims=True) / (2.0 * sq + EPS)

        down = coef(1)
        weight = down if weight is None else weight * down
        if 2 * bit < count:
            gram = down * gram * coef(0)
            gram = gram + jnp.where(
                row & bit == 0, pltpu.roll(gram, count - bit, 0), pltpu.roll(gram, bit, 0)
            )
            lanes = gram.shape[1]
            gram = gram + jnp.where(
                lane & bit == 0, pltpu.roll(gram, lanes - bit, 1), pltpu.roll(gram, bit, 1)
            )
        bit *= 2
    return weight


def kernel(
    sections, replicas, cols,
    act_hbm, pre_hbm, up_hbm, weights_hbm,
    passed_ref, combined_ref,
    act_v, pre_v, up_v, kernel_v, act_t, grad_v, grad_tiles,
    act_in, grad_in, patches, blocks, pair_sums, gram_in, merged, merged_in, shifted, igrad,
    load_sem, act_send, act_recv, grad_send, grad_recv, gram_send, gram_recv,
    merged_send, merged_recv, pass_sem, combined_v, zeros_v, out_sem,
):
    pixels, channels = act_v.shape
    part = channels // 4
    lanes = 128
    unit = channels // replicas
    pipe, rep = lax.axis_index("pipe"), lax.axis_index("rep")
    z, y = rep // 2, rep % 2
    half, near, across, far = roles(z, y, rep)
    outer = (z == 0) | (z == 3)
    inner = (z == 1) | (z == 2)
    quarter = half * 2 + y

    barrier = pltpu.get_barrier_semaphore()
    for step in range(1, replicas):
        peer = lax.rem(rep + step, replicas)
        pl.semaphore_signal(barrier, inc=1, device_id=(pipe, peer), device_id_type=MESH)

    @pl.when(pipe < sections - 1)
    def _():
        pl.semaphore_signal(barrier, inc=1, device_id=(pipe + 1, rep), device_id_type=MESH)

    loads = [
        pltpu.make_async_copy(src, dst, load_sem.at[n])
        for n, (src, dst) in enumerate(
            ((act_hbm, act_v), (pre_hbm, pre_v), (up_hbm, up_v), (weights_hbm, kernel_v))
        )
    ]
    for load in loads:
        load.start()

    def index(zz, yy):
        return zz * 2 + yy

    def remote(src, dst, send, recv, target):
        return pltpu.make_async_remote_copy(
            src_ref=src, dst_ref=dst, send_sem=send, recv_sem=recv,
            device_id=(pipe, target), device_id_type=MESH,
        )

    def act_own(slot, block_of, target):
        rows = pl.ds(pl.multiple_of(block_of * part, part), part)
        return remote(act_t.at[rows, :], act_in.at[rep], act_send.at[slot], act_recv.at[rep], target)

    def act_pass(slot, block):
        return remote(
            act_in.at[block], act_in.at[block], act_send.at[slot], act_recv.at[block], index(near, y)
        )

    def grad_copy(slot, i, src, block, target):
        return remote(
            src, grad_in.at[block, i], grad_send.at[slot, i], grad_recv.at[block, i], target
        )

    other_inner = 2 - half
    own_acts = (
        (0, quarter, index(near, y)),
        (1, half * 2 + 1 - y, index(z, 1 - y)),
        (2, (1 - half) * 2 + y, index(other_inner, y)),
        (3, (1 - half) * 2 + 1 - y, index(other_inner, 1 - y)),
    )
    order = [
        index(z, y), index(z, 1 - y), index(near, y), index(across, y),
        index(near, 1 - y), index(across, 1 - y), index(far, y), index(far, 1 - y),
    ]

    sent = []

    def start(cond, copies):
        if cond is None:
            for copy in copies:
                copy().start()
        else:
            @pl.when(cond)
            def _():
                for copy in copies:
                    copy().start()
        sent.append((cond, copies))

    def wait_act(block):
        act_pass(4, block).wait_recv()

    def wait_grad(block):
        grad_copy(0, 0, grad_in.at[block, 0], block, rep).wait_recv()

        @pl.when(inner)
        def _():
            grad_copy(0, 1, grad_in.at[block, 1], block, rep).wait_recv()

    def own_grad(slot, tiles, target):
        return [
            functools.partial(grad_copy, slot, i, grad_tiles.at[tile], rep, target)
            for i, tile in enumerate(tiles)
        ]

    def pass_grad(slot, block, target, extra=None):
        start(None, [functools.partial(grad_copy, slot, 0, grad_in.at[block, 0], block, target)])
        start(inner, [functools.partial(grad_copy, slot, 1, grad_in.at[block, 1], block, target)])

    def patch(block):
        tile = act_in[block].astype(F32)
        pixel = lax.broadcasted_iota(jnp.int32, (1, pixels), 1)
        column = pixel % cols
        for j in range(3):
            if j == 1:
                moved = tile
            else:
                moved = pltpu.roll(tile, (1 - j) % pixels, 1)
                moved = jnp.where(column > 0 if j == 0 else column < cols - 1, moved, 0.0)
            for i in range(3):
                if i == 1:
                    placed = moved
                else:
                    placed = pltpu.roll(moved, ((1 - i) * cols) % pixels, 1)
                    placed = jnp.where(
                        pixel >= cols if i == 0 else pixel < pixels - cols, placed, 0.0
                    )
                patches[block, pl.ds((i * 3 + j) * part, part), :] = placed.astype(BF16)

    def multiply(k):
        block = order[k]
        grad = jnp.concatenate([grad_in[block, 0], grad_in[block, 1]], axis=1)

        for i in range(3):
            rows = pl.ds(3 * i * part, 3 * part)
            blocks[block, rows, :] = jnp.dot(
                patches[block, rows, :], grad, preferred_element_type=F32
            )

        def step(t, sums):
            here = pl.ds(pl.multiple_of(t * part, part), part)
            new = blocks[block, here, :]
            out = []
            for m in range(k + 1):
                against = new if m == k else blocks[order[m], here, :]
                folded = fold(new * against)
                out.append(sums[m] + folded[:, :lanes] + folded[:, lanes:])
            return tuple(out)

        zero = jnp.zeros((8, lanes), F32)
        sums = lax.fori_loop(0, 9, step, (zero,) * (k + 1), unroll=3)
        for m in range(k + 1):
            total = jnp.sum(sums[m], axis=0, keepdims=True)
            pair_sums[order[m], pl.ds(block, 1), :] = total
            if m < k:
                pair_sums[block, pl.ds(order[m], 1), :] = total

    loads[0].wait()
    act_t[...] = act_v[...].T
    pl.semaphore_wait(barrier, replicas - 1 + (pipe > 0).astype(jnp.int32))
    start(None, [functools.partial(act_own, *args) for args in own_acts])
    loads[1].wait()
    loads[2].wait()
    z_f = pre_v[...].astype(F32)
    sig = jax.nn.sigmoid(z_f)
    grad = (up_v[...].astype(F32) * sig * (1.0 + z_f * (1.0 - sig))).astype(BF16)
    grad_v[...] = grad
    for tile in range(3):
        grad_tiles[tile] = grad[:, tile * lanes : (tile + 1) * lanes]
    start(inner, own_grad(1, (1, 2), index(across, y)))
    start(outer, own_grad(1, (1, 2), index(near, y)))
    start(inner, own_grad(0, (1, 2), index(z, 1 - y)))
    start(outer, own_grad(0, (0,), index(z, 1 - y)))
    start(outer, own_grad(2, (0,), index(far, y)))
    start(inner, own_grad(2, (0,), index(near, y)))
    start(inner, own_grad(3, (0,), index(far, y)))

    act_in[rep] = act_t[pl.ds(pl.multiple_of(quarter * part, part), part), :]

    @pl.when(outer)
    def _():
        grad_in[rep, 0] = grad_tiles[0]
        for block in range(replicas):
            grad_in[block, 1] = jnp.zeros((pixels, lanes), BF16)

    @pl.when(inner)
    def _():
        grad_in[rep, 0] = grad_tiles[1]
        grad_in[rep, 1] = grad_tiles[2]

    def relay(slot, k):
        @pl.when(inner)
        def _():
            wait_act(order[k])

        start(inner, [functools.partial(act_pass, slot, order[k])])

    def take(k, relayed):
        if relayed:
            @pl.when(outer)
            def _():
                wait_act(order[k])
        else:
            wait_act(order[k])
        patch(order[k])

    patch(rep)
    multiply(0)
    wait_act(order[1])
    start(None, [functools.partial(act_pass, 4, order[1])])
    relay(5, 3)
    relay(6, 5)
    patch(order[1])
    wait_grad(order[2])
    pass_grad(4, order[2], index(z, 1 - y))
    start(inner, [
        functools.partial(grad_copy, 5, i, grad_in.at[order[2], i], order[2], index(across, y))
        for i in range(2)
    ])
    relay(7, 6)
    relay(8, 7)
    wait_grad(order[1])
    multiply(1)
    wait_grad(order[3])
    pass_grad(6, order[3], index(z, 1 - y))
    take(2, False)
    multiply(2)
    take(3, True)
    multiply(3)
    take(4, False)
    take(5, True)
    wait_grad(order[4])
    multiply(4)
    wait_grad(order[6])
    pass_grad(7, order[6], index(z, 1 - y))
    wait_grad(order[5])
    multiply(5)
    take(6, True)
    multiply(6)
    take(7, True)
    wait_grad(order[7])
    multiply(7)

    lane = lax.broadcasted_iota(jnp.int32, (replicas, lanes), 1)
    gram = jnp.zeros((replicas, lanes), F32)
    for block in range(replicas):
        gram = jnp.where(lane == block, jnp.sum(pair_sums[block], axis=1, keepdims=True), gram)
    gram_in[rep] = gram

    def gram_copy(step):
        peer = lax.rem(rep + step, replicas)
        return remote(gram_in.at[rep], gram_in.at[rep], gram_send.at[step], gram_recv.at[rep], peer)

    def gram_from(step):
        peer = lax.rem(rep + step, replicas)
        return remote(gram_in.at[peer], gram_in.at[peer], gram_send.at[step], gram_recv.at[peer], peer)

    for step in range(1, replicas):
        start(None, [functools.partial(gram_copy, step)])

    edge = jnp.zeros((cols, channels), BF16)
    for j in range(3):
        shifted[j, pl.ds(0, cols), :] = edge
        shifted[j, pl.ds(cols + pixels, cols), :] = edge
    grad = grad_v[...].astype(F32)
    column = lax.broadcasted_iota(jnp.int32, (pixels, channels), 0) % cols
    here = pl.ds(cols, pixels)
    shifted[0, here, :] = jnp.where(column < cols - 1, pltpu.roll(grad, pixels - 1, 0), 0.0).astype(BF16)
    shifted[1, here, :] = grad_v[...]
    shifted[2, here, :] = jnp.where(column > 0, pltpu.roll(grad, 1, 0), 0.0).astype(BF16)
    loads[3].wait()
    total = jnp.zeros((pixels, channels), F32)
    for i in range(3):
        for j in range(3):
            total = total + lax.dot_general(
                shifted[j, pl.ds((2 - i) * cols, pixels), :],
                kernel_v[pl.ds((i * 3 + j) * channels, channels), :],
                (((1,), (1,)), ((), ())),
                preferred_element_type=F32,
            )
    igrad[...] = total.astype(BF16)

    nothing = pltpu.make_async_copy(zeros_v, passed_ref, load_sem.at[4])

    @pl.when(pipe == sections - 1)
    def _():
        zeros_v[...] = jnp.zeros_like(zeros_v)
        nothing.start()

    passing = pltpu.make_async_remote_copy(
        src_ref=igrad,
        dst_ref=passed_ref,
        send_sem=pass_sem.at[0],
        recv_sem=pass_sem.at[1],
        device_id=(jnp.maximum(pipe - 1, 0), rep),
        device_id_type=MESH,
    )

    @pl.when(pipe > 0)
    def _():
        passing.start()

    for step in range(1, replicas):
        gram_from(step).wait_recv()
    gram = gram_in[0]
    for block in range(1, replicas):
        gram = gram + gram_in[block]
    weight = adasum_weights(gram)

    def merged_copy(t, cb, wide, owner, local):
        src = merged.at[t, cb] if wide else merged.at[t, cb, pl.ds(0, 1)]
        dst = merged_in.at[local, pl.ds(1, 2)] if wide else merged_in.at[local, pl.ds(0, 1)]
        kind = 1 if wide else 0
        return remote(src, dst, merged_send.at[t, cb], merged_recv.at[local, kind], owner)

    for t in range(9):
        tap = t + (1 - half) * (8 - 2 * t)
        here = pl.ds(pl.multiple_of(tap * part, part), part)
        total = weight[0:1, 0:1] * blocks[0, here, :]
        for block in range(1, replicas):
            total = total + weight[block : block + 1, 0:1] * blocks[block, here, :]
        total = total.astype(BF16)
        for cb in range(2):
            rows = slice(cb * unit, (cb + 1) * unit)
            merged[t, cb, 0] = total[rows, :lanes]
            merged[t, cb, 1] = total[rows, lanes:]
            place = tap * replicas + quarter * 2 + cb
            owner, local = place // 9, place % 9
            mine = owner == rep

            @pl.when(mine & outer)
            def _():
                merged_in[local, 0] = merged[t, cb, 0]

            @pl.when(mine & inner)
            def _():
                merged_in[local, 1] = merged[t, cb, 0]
                merged_in[local, 2] = merged[t, cb, 1]

            away = owner != rep
            start(away & outer, [functools.partial(merged_copy, t, cb, False, owner, local)])
            start(away & inner, [functools.partial(merged_copy, t, cb, True, owner, local)])

    def out_copy(local):
        rows = pl.ds(local * unit * 3, unit * 3)
        return pltpu.make_async_copy(
            combined_v.at[rows, :], combined_ref.at[rows, :], out_sem.at[local]
        )

    for local in range(9):
        place = rep * 9 + local
        of = (place % replicas) // 2
        its_half, its_y = of // 2, of % 2
        for wide, plane in ((False, 3 * its_half), (True, 1 + its_half)):
            @pl.when(index(plane, its_y) != rep)
            def _():
                merged_copy(0, 0, wide, rep, local).wait_recv()
        for tile in range(3):
            at = pl.ds(local * unit * 3 + tile, unit, stride=3)
            combined_v[at, :] = merged_in[local, tile].astype(F32)
        written = out_copy(local)
        written.start()

    for cond, copies in sent:
        if cond is None:
            for copy in copies:
                copy().wait_send()
        else:
            @pl.when(cond)
            def _():
                for copy in copies:
                    copy().wait_send()

    for local in range(9):
        out_copy(local).wait()

    @pl.when(pipe > 0)
    def _():
        passing.wait_send()

    @pl.when(pipe < sections - 1)
    def _():
        passing.wait_recv()

    @pl.when(pipe == sections - 1)
    def _():
        nothing.wait()


def update(
    pieces, combined, master, momentum, passed_in, new_momentum, new_weights, passed_out,
    combined_v, master_v, momentum_v, moved_v, weights_v, sem, passed_v, passed_sem,
):
    rows = combined.shape[0] // pieces

    def copy(n, src, dst, piece):
        here = pl.ds(piece * rows, rows)
        return pltpu.make_async_copy(src.at[here, :], dst.at[here, :], sem.at[n, piece])

    def reads(piece):
        return (
            copy(0, combined, combined_v, piece),
            copy(1, momentum, momentum_v, piece),
            copy(2, master, master_v, piece),
        )

    def writes(piece):
        return (copy(3, moved_v, new_momentum, piece), copy(4, weights_v, new_weights, piece))

    for piece in range(pieces):
        for read in reads(piece):
            read.start()
    arriving = pltpu.make_async_copy(passed_in, passed_v, passed_sem.at[0])
    leaving = pltpu.make_async_copy(passed_v, passed_out, passed_sem.at[1])
    arriving.start()
    for piece in range(pieces):
        here = pl.ds(piece * rows, rows)
        for read in reads(piece):
            read.wait()
        moved = 0.9 * momentum_v[here, :] + 0.0625 * combined_v[here, :]
        moved_v[here, :] = moved
        weights_v[here, :] = master_v[here, :] - 0.02 * moved
        for write in writes(piece):
            write.start()
        if piece == 0:
            arriving.wait()
            leaving.start()
    leaving.wait()
    for piece in range(pieces):
        for write in writes(piece):
            write.wait()


def factor_body(sections, replicas, activations, preactivation, upstream, weights, master, momentum):
    tile = activations.shape[3:]
    cols, channels = tile[1], tile[2]
    pixels = tile[0] * cols
    taps_rows = weights.shape[1]
    lanes = 128
    part, unit = channels // 4, channels // replicas
    flat = (momentum.shape[2] // lanes, lanes)
    big = pl.BlockSpec(memory_space=pl.ANY)
    passed, combined = pl.pallas_call(
        functools.partial(kernel, sections, replicas, cols),
        out_shape=(
            jax.ShapeDtypeStruct((pixels, channels), BF16),
            jax.ShapeDtypeStruct(flat, F32),
        ),
        in_specs=[big] * 4,
        out_specs=(big, big),
        scratch_shapes=[
            pltpu.VMEM((pixels, channels), BF16),
            pltpu.VMEM((pixels, channels), BF16),
            pltpu.VMEM((pixels, channels), BF16),
            pltpu.VMEM((taps_rows, channels), BF16),
            pltpu.VMEM((channels, pixels), BF16),
            pltpu.VMEM((pixels, channels), BF16),
            pltpu.VMEM((3, pixels, lanes), BF16),
            pltpu.VMEM((replicas, part, pixels), BF16),
            pltpu.VMEM((replicas, 2, pixels, lanes), BF16),
            pltpu.VMEM((replicas, 9 * part, pixels), BF16),
            pltpu.VMEM((replicas, 9 * part, 2 * lanes), F32),
            pltpu.VMEM((replicas, replicas, lanes), F32),
            pltpu.VMEM((replicas, replicas, lanes), F32),
            pltpu.VMEM((9, 2, 2, unit, lanes), BF16),
            pltpu.VMEM((9, 3, unit, lanes), BF16),
            pltpu.VMEM((3, pixels + 2 * cols, channels), BF16),
            pltpu.VMEM((pixels, channels), BF16),
            pltpu.SemaphoreType.DMA((5,)),
            pltpu.SemaphoreType.DMA((9,)),
            pltpu.SemaphoreType.DMA((replicas,)),
            pltpu.SemaphoreType.DMA((8, 2)),
            pltpu.SemaphoreType.DMA((replicas, 2)),
            pltpu.SemaphoreType.DMA((replicas,)),
            pltpu.SemaphoreType.DMA((replicas,)),
            pltpu.SemaphoreType.DMA((9, 2)),
            pltpu.SemaphoreType.DMA((9, 2)),
            pltpu.SemaphoreType.DMA((2,)),
            pltpu.VMEM(flat, F32),
            pltpu.VMEM((pixels, channels), BF16),
            pltpu.SemaphoreType.DMA((9,)),
        ],
        compiler_params=pltpu.CompilerParams(
            collective_id=0, has_side_effects=True, vmem_limit_bytes=60 * 1024 * 1024
        ),
    )(
        activations.reshape(pixels, channels),
        preactivation.reshape(pixels, channels),
        upstream.reshape(pixels, channels),
        weights[0],
    )
    pieces = next(n for n in (1,) if flat[0] % (8 * n) == 0)
    new_momentum, new_weights, passed = pl.pallas_call(
        functools.partial(update, pieces),
        out_shape=(
            jax.ShapeDtypeStruct(flat, F32),
            jax.ShapeDtypeStruct(flat, F32),
            jax.ShapeDtypeStruct((pixels, channels), BF16),
        ),
        in_specs=[big] * 4,
        out_specs=(big,) * 3,
        scratch_shapes=[pltpu.VMEM(flat, F32)] * 5
        + [
            pltpu.SemaphoreType.DMA((5, pieces)),
            pltpu.VMEM((pixels, channels), BF16),
            pltpu.SemaphoreType.DMA((2,)),
        ],
    )(combined, master.reshape(flat), momentum.reshape(flat), passed)
    return (
        passed.reshape(activations.shape),
        new_momentum.reshape(momentum.shape),
        new_weights.reshape(master.shape),
    )


def pick(sections, replicas, *arrays):
    activations, weights, momentum = arrays[0], arrays[3], arrays[5]
    channels = activations.shape[5]
    fits = (
        replicas == 8
        and activations.shape[2] == 1
        and weights.shape[1] == 9 * channels
        and weights.shape[2] == channels
        and channels == 3 * 128
        and (activations.shape[3] * activations.shape[4]) % 128 == 0
        and activations.shape[4] % 16 == 0
        and momentum.shape[2] % 1024 == 0
    )
    return factor_body(sections, replicas, *arrays) if fits else body(*arrays)


def solution(mesh):
    return jax.shard_map(
        functools.partial(pick, mesh.shape["pipe"], mesh.shape["rep"]),
        mesh=mesh,
        in_specs=(
            P("pipe", "rep", None, None, None, None),
            P("pipe", "rep", None, None, None, None),
            P("pipe", "rep", None, None, None, None),
            P("pipe", None, None),
            P("pipe", "rep", None),
            P("pipe", "rep", None),
        ),
        out_specs=(
            P("pipe", "rep", None, None, None, None),
            P("pipe", "rep", None),
            P("pipe", "rep", None),
        ),
        check_vma=False,
    )
```

```python
import functools

import jax
import jax.numpy as jnp
from jax import lax
from jax.experimental import pallas as pl
from jax.experimental.pallas import tpu as pltpu
from jax.sharding import PartitionSpec as P

EPS = 1e-06


def swapped(shard, axis, stride):
    return lax.ppermute(shard, axis, [(i, i ^ 1 << stride) for i in range(lax.axis_size(axis))])


def from_behind(shard, axis, by):
    count = lax.axis_size(axis)
    pairs = [(i, i + by) for i in range(count) if 0 <= i + by < count]
    return lax.ppermute(shard, axis, pairs)


def shifted_patches(tile_data, flipped):
    frames, tile_rows, tile_cols, channels = tile_data.shape
    padded = jnp.pad(tile_data, ((0, 0), (1, 1), (1, 1), (0, 0)))
    if flipped:
        offsets = [(2 - row_off, 2 - col_off) for row_off in range(3) for col_off in range(3)]
    else:
        offsets = [(row_off, col_off) for row_off in range(3) for col_off in range(3)]
    pieces = [
        padded[:, first : first + tile_rows, second : second + tile_cols, :]
        for first, second in offsets
    ]
    return jnp.concatenate(pieces, axis=-1).reshape(frames * tile_rows * tile_cols, 9 * channels)


def local_backward(tile_data, preact_tile, upstream_tile, kernel):
    frames, tile_rows, tile_cols, channels = tile_data.shape
    pre_float = preact_tile.astype(jnp.float32)
    sigmoid_val = jax.nn.sigmoid(pre_float)
    local_grad = (
        upstream_tile.astype(jnp.float32) * sigmoid_val * (1.0 + pre_float * (1.0 - sigmoid_val))
    ).astype(jnp.bfloat16)
    flat_grad = local_grad.reshape(-1, channels)
    patches = shifted_patches(tile_data, False)
    weight_grad = lax.dot_general(
        patches, flat_grad, (((0,), (0,)), ((), ())), preferred_element_type=jnp.float32
    ).astype(jnp.bfloat16)
    grad_patches = shifted_patches(local_grad, True).reshape(-1, 9, channels)
    kernel_taps = kernel.reshape(9, channels, channels)
    summed = lax.dot_general(
        grad_patches, kernel_taps, (((1, 2), (0, 2)), ((), ())), preferred_element_type=jnp.float32
    )
    return (
        weight_grad,
        summed.astype(jnp.bfloat16).reshape(frames, tile_rows, tile_cols, channels),
    )


def group_sum(partials, sum_bits):
    for bit_number in range(sum_bits):
        partials = partials + swapped(partials, "rep", bit_number)
    return partials


def body(activations, preactivation, upstream, weights, master, momentum):
    weight_grad, input_grad = local_backward(
        activations[0, 0], preactivation[0, 0], upstream[0, 0], weights[0]
    )
    passed = from_behind(input_grad, "pipe", -1)
    replicas = lax.axis_size("rep")
    level_count = replicas.bit_length() - 1
    rep_index = lax.axis_index("rep")
    held_rows = weight_grad.reshape(replicas, -1)
    for level_num in range(level_count):
        is_lower = jnp.right_shift(rep_index, level_num) & 1 == 0
        paired = held_rows.reshape(-1, 2, held_rows.shape[1])
        keep_rows = jnp.where(is_lower, paired[:, 0], paired[:, 1])
        give_rows = jnp.where(is_lower, paired[:, 1], paired[:, 0])
        other_rows = swapped(give_rows, "rep", level_num)
        keep_float = keep_rows.astype(jnp.float32)
        other_float = other_rows.astype(jnp.float32)
        keep_sq = jnp.sum(keep_float * keep_float)
        other_sq = jnp.sum(other_float * other_float)
        partials = jnp.stack(
            [
                jnp.where(is_lower, keep_sq, other_sq),
                jnp.where(is_lower, other_sq, keep_sq),
                jnp.sum(keep_float * other_float),
            ]
        )
        sum_bits = level_num + 1
        partials = group_sum(partials, sum_bits)
        lower_coef = 1.0 - partials[2] / (2.0 * partials[0] + EPS)
        upper_coef = 1.0 - partials[2] / (2.0 * partials[1] + EPS)
        keep_coef = jnp.where(is_lower, lower_coef, upper_coef)
        other_coef = jnp.where(is_lower, upper_coef, lower_coef)
        merged = keep_coef * keep_rows.astype(jnp.float32) + other_coef * other_rows.astype(
            jnp.float32
        )
        held_rows = merged.astype(jnp.bfloat16)
    combined = held_rows.astype(jnp.float32).reshape(momentum.shape)
    new_momentum = 0.9 * momentum + 0.0625 * combined
    new_weights = master - 0.02 * new_momentum
    return (passed[None, None], new_momentum, new_weights)


MESH = pl.DeviceIdType.MESH
F32 = jnp.float32
BF16 = jnp.bfloat16


def fold(product):
    return jnp.sum(product.reshape(-1, 8, product.shape[-1]), axis=0)


def roles(z, y, rep):
    half = z // 2
    near = z + 1 - 2 * (z % 2)
    across = 2 - half
    far = 3 - 3 * half
    return half, near, across, far


def adasum_weights(gram):
    count = gram.shape[0]
    row = lax.broadcasted_iota(jnp.int32, gram.shape, 0)
    lane = lax.broadcasted_iota(jnp.int32, gram.shape, 1)
    weight = None
    bit = 1
    while bit < count:
        own = jnp.where(lane == row, gram, 0.0)
        cross = jnp.where(lane == row ^ bit, gram, 0.0)

        def coef(axis):
            sq = jnp.maximum(jnp.sum(own, axis=axis, keepdims=True), 0.0)
            return 1.0 - jnp.sum(cross, axis=axis, keepdims=True) / (2.0 * sq + EPS)

        down = coef(1)
        weight = down if weight is None else weight * down
        if 2 * bit < count:
            gram = down * gram * coef(0)
            gram = gram + jnp.where(
                row & bit == 0, pltpu.roll(gram, count - bit, 0), pltpu.roll(gram, bit, 0)
            )
            lanes = gram.shape[1]
            gram = gram + jnp.where(
                lane & bit == 0, pltpu.roll(gram, lanes - bit, 1), pltpu.roll(gram, bit, 1)
            )
        bit *= 2
    return weight


def kernel(
    sections, replicas, cols,
    act_hbm, pre_hbm, up_hbm, weights_hbm, master_hbm, momentum_hbm,
    passed_ref, new_momentum, new_weights,
    act_v, pre_v, up_v, kernel_v, act_t, grad_v, grad_tiles,
    act_in, grad_in, patches, blocks, pair_sums, gram_in, merged, merged_in, shifted, igrad,
    load_sem, act_send, act_recv, grad_send, grad_recv, gram_send, gram_recv,
    merged_send, merged_recv, pass_sem, master_v, momentum_v,
):
    pixels, channels = act_v.shape
    part = channels // 4
    lanes = 128
    unit = channels // replicas
    pipe, rep = lax.axis_index("pipe"), lax.axis_index("rep")
    z, y = rep // 2, rep % 2
    half, near, across, far = roles(z, y, rep)
    outer = (z == 0) | (z == 3)
    inner = (z == 1) | (z == 2)
    quarter = half * 2 + y

    barrier = pltpu.get_barrier_semaphore()
    for step in range(1, replicas):
        peer = lax.rem(rep + step, replicas)
        pl.semaphore_signal(barrier, inc=1, device_id=(pipe, peer), device_id_type=MESH)

    @pl.when(pipe < sections - 1)
    def _():
        pl.semaphore_signal(barrier, inc=1, device_id=(pipe + 1, rep), device_id_type=MESH)

    loads = [
        pltpu.make_async_copy(src, dst, load_sem.at[n])
        for n, (src, dst) in enumerate(
            (
                (act_hbm, act_v), (pre_hbm, pre_v), (up_hbm, up_v), (weights_hbm, kernel_v),
                (master_hbm, master_v), (momentum_hbm, momentum_v),
            )
        )
    ]
    for load in loads:
        load.start()

    def index(zz, yy):
        return zz * 2 + yy

    def remote(src, dst, send, recv, target):
        return pltpu.make_async_remote_copy(
            src_ref=src, dst_ref=dst, send_sem=send, recv_sem=recv,
            device_id=(pipe, target), device_id_type=MESH,
        )

    def act_own(slot, block_of, target):
        rows = pl.ds(pl.multiple_of(block_of * part, part), part)
        return remote(act_t.at[rows, :], act_in.at[rep], act_send.at[slot], act_recv.at[rep], target)

    def act_pass(slot, block):
        return remote(
            act_in.at[block], act_in.at[block], act_send.at[slot], act_recv.at[block], index(near, y)
        )

    def grad_copy(slot, i, src, block, target):
        return remote(
            src, grad_in.at[block, i], grad_send.at[slot, i], grad_recv.at[block, i], target
        )

    other_inner = 2 - half
    own_acts = (
        (0, quarter, index(near, y)),
        (1, half * 2 + 1 - y, index(z, 1 - y)),
        (2, (1 - half) * 2 + y, index(other_inner, y)),
        (3, (1 - half) * 2 + 1 - y, index(other_inner, 1 - y)),
    )
    order = [
        index(z, y), index(z, 1 - y), index(near, y), index(across, y),
        index(near, 1 - y), index(across, 1 - y), index(far, y), index(far, 1 - y),
    ]

    sent = []

    def start(cond, copies):
        if cond is None:
            for copy in copies:
                copy().start()
        else:
            @pl.when(cond)
            def _():
                for copy in copies:
                    copy().start()
        sent.append((cond, copies))

    def wait_act(block):
        act_pass(4, block).wait_recv()

    def wait_grad(block):
        grad_copy(0, 0, grad_in.at[block, 0], block, rep).wait_recv()

        @pl.when(inner)
        def _():
            grad_copy(0, 1, grad_in.at[block, 1], block, rep).wait_recv()

    def own_grad(slot, tiles, target):
        return [
            functools.partial(grad_copy, slot, i, grad_tiles.at[tile], rep, target)
            for i, tile in enumerate(tiles)
        ]

    def pass_grad(slot, block, target, extra=None):
        start(None, [functools.partial(grad_copy, slot, 0, grad_in.at[block, 0], block, target)])
        start(inner, [functools.partial(grad_copy, slot, 1, grad_in.at[block, 1], block, target)])

    def patch(block):
        tile = act_in[block].astype(F32)
        pixel = lax.broadcasted_iota(jnp.int32, (1, pixels), 1)
        column = pixel % cols
        for j in range(3):
            if j == 1:
                moved = tile
            else:
                moved = pltpu.roll(tile, (1 - j) % pixels, 1)
                moved = jnp.where(column > 0 if j == 0 else column < cols - 1, moved, 0.0)
            for i in range(3):
                if i == 1:
                    placed = moved
                else:
                    placed = pltpu.roll(moved, ((1 - i) * cols) % pixels, 1)
                    placed = jnp.where(
                        pixel >= cols if i == 0 else pixel < pixels - cols, placed, 0.0
                    )
                patches[block, pl.ds((i * 3 + j) * part, part), :] = placed.astype(BF16)

    def multiply(k):
        block = order[k]
        grad = jnp.concatenate([grad_in[block, 0], grad_in[block, 1]], axis=1)

        for i in range(3):
            rows = pl.ds(3 * i * part, 3 * part)
            blocks[block, rows, :] = jnp.dot(
                patches[block, rows, :], grad, preferred_element_type=F32
            )

        def step(t, sums):
            here = pl.ds(pl.multiple_of(t * part, part), part)
            new = blocks[block, here, :]
            out = []
            for m in range(k + 1):
                against = new if m == k else blocks[order[m], here, :]
                folded = fold(new * against)
                out.append(sums[m] + folded[:, :lanes] + folded[:, lanes:])
            return tuple(out)

        zero = jnp.zeros((8, lanes), F32)
        sums = lax.fori_loop(0, 9, step, (zero,) * (k + 1), unroll=3)
        for m in range(k + 1):
            total = jnp.sum(sums[m], axis=0, keepdims=True)
            pair_sums[order[m], pl.ds(block, 1), :] = total
            if m < k:
                pair_sums[block, pl.ds(order[m], 1), :] = total

    loads[0].wait()
    act_t[...] = act_v[...].T
    pl.semaphore_wait(barrier, replicas - 1 + (pipe > 0).astype(jnp.int32))
    start(None, [functools.partial(act_own, *args) for args in own_acts])
    loads[1].wait()
    loads[2].wait()
    z_f = pre_v[...].astype(F32)
    sig = jax.nn.sigmoid(z_f)
    grad = (up_v[...].astype(F32) * sig * (1.0 + z_f * (1.0 - sig))).astype(BF16)
    grad_v[...] = grad
    for tile in range(3):
        grad_tiles[tile] = grad[:, tile * lanes : (tile + 1) * lanes]
    start(inner, own_grad(1, (1, 2), index(across, y)))
    start(outer, own_grad(1, (1, 2), index(near, y)))
    start(inner, own_grad(0, (1, 2), index(z, 1 - y)))
    start(outer, own_grad(0, (0,), index(z, 1 - y)))
    start(outer, own_grad(2, (0,), index(far, y)))
    start(inner, own_grad(2, (0,), index(near, y)))
    start(inner, own_grad(3, (0,), index(far, y)))

    act_in[rep] = act_t[pl.ds(pl.multiple_of(quarter * part, part), part), :]

    @pl.when(outer)
    def _():
        grad_in[rep, 0] = grad_tiles[0]
        for block in range(replicas):
            grad_in[block, 1] = jnp.zeros((pixels, lanes), BF16)

    @pl.when(inner)
    def _():
        grad_in[rep, 0] = grad_tiles[1]
        grad_in[rep, 1] = grad_tiles[2]

    def relay(slot, k):
        @pl.when(inner)
        def _():
            wait_act(order[k])

        start(inner, [functools.partial(act_pass, slot, order[k])])

    def take(k, relayed):
        if relayed:
            @pl.when(outer)
            def _():
                wait_act(order[k])
        else:
            wait_act(order[k])
        patch(order[k])

    patch(rep)
    multiply(0)
    wait_act(order[1])
    start(None, [functools.partial(act_pass, 4, order[1])])
    relay(5, 3)
    relay(6, 5)
    patch(order[1])
    wait_grad(order[2])
    pass_grad(4, order[2], index(z, 1 - y))
    start(inner, [
        functools.partial(grad_copy, 5, i, grad_in.at[order[2], i], order[2], index(across, y))
        for i in range(2)
    ])
    relay(7, 6)
    relay(8, 7)
    wait_grad(order[1])
    multiply(1)
    wait_grad(order[3])
    pass_grad(6, order[3], index(z, 1 - y))
    take(2, False)
    multiply(2)
    take(3, True)
    multiply(3)
    take(4, False)
    take(5, True)
    wait_grad(order[4])
    multiply(4)
    wait_grad(order[6])
    pass_grad(7, order[6], index(z, 1 - y))
    wait_grad(order[5])
    multiply(5)
    take(6, True)
    multiply(6)
    take(7, True)
    wait_grad(order[7])
    multiply(7)

    lane = lax.broadcasted_iota(jnp.int32, (replicas, lanes), 1)
    gram = jnp.zeros((replicas, lanes), F32)
    for block in range(replicas):
        gram = jnp.where(lane == block, jnp.sum(pair_sums[block], axis=1, keepdims=True), gram)
    gram_in[rep] = gram

    def gram_copy(step):
        peer = lax.rem(rep + step, replicas)
        return remote(gram_in.at[rep], gram_in.at[rep], gram_send.at[step], gram_recv.at[rep], peer)

    def gram_from(step):
        peer = lax.rem(rep + step, replicas)
        return remote(gram_in.at[peer], gram_in.at[peer], gram_send.at[step], gram_recv.at[peer], peer)

    for step in range(1, replicas):
        start(None, [functools.partial(gram_copy, step)])

    edge = jnp.zeros((cols, channels), BF16)
    for j in range(3):
        shifted[j, pl.ds(0, cols), :] = edge
        shifted[j, pl.ds(cols + pixels, cols), :] = edge
    grad = grad_v[...].astype(F32)
    column = lax.broadcasted_iota(jnp.int32, (pixels, channels), 0) % cols
    here = pl.ds(cols, pixels)
    shifted[0, here, :] = jnp.where(column < cols - 1, pltpu.roll(grad, pixels - 1, 0), 0.0).astype(BF16)
    shifted[1, here, :] = grad_v[...]
    shifted[2, here, :] = jnp.where(column > 0, pltpu.roll(grad, 1, 0), 0.0).astype(BF16)
    loads[3].wait()
    total = jnp.zeros((pixels, channels), F32)
    for i in range(3):
        for j in range(3):
            total = total + lax.dot_general(
                shifted[j, pl.ds((2 - i) * cols, pixels), :],
                kernel_v[pl.ds((i * 3 + j) * channels, channels), :],
                (((1,), (1,)), ((), ())),
                preferred_element_type=F32,
            )
    igrad[...] = total.astype(BF16)

    @pl.when(pipe == sections - 1)
    def _():
        passed_ref[...] = jnp.zeros_like(passed_ref)

    passing = pltpu.make_async_remote_copy(
        src_ref=igrad,
        dst_ref=passed_ref,
        send_sem=pass_sem.at[0],
        recv_sem=pass_sem.at[1],
        device_id=(jnp.maximum(pipe - 1, 0), rep),
        device_id_type=MESH,
    )

    @pl.when(pipe > 0)
    def _():
        passing.start()

    for step in range(1, replicas):
        gram_from(step).wait_recv()
    gram = gram_in[0]
    for block in range(1, replicas):
        gram = gram + gram_in[block]
    weight = adasum_weights(gram)

    def merged_copy(t, cb, wide, owner, local):
        src = merged.at[t, cb] if wide else merged.at[t, cb, pl.ds(0, 1)]
        dst = merged_in.at[local, pl.ds(1, 2)] if wide else merged_in.at[local, pl.ds(0, 1)]
        kind = 1 if wide else 0
        return remote(src, dst, merged_send.at[t, cb], merged_recv.at[local, kind], owner)

    for t in range(9):
        tap = t + (1 - half) * (8 - 2 * t)
        here = pl.ds(pl.multiple_of(tap * part, part), part)
        total = weight[0:1, 0:1] * blocks[0, here, :]
        for block in range(1, replicas):
            total = total + weight[block : block + 1, 0:1] * blocks[block, here, :]
        total = total.astype(BF16)
        for cb in range(2):
            rows = slice(cb * unit, (cb + 1) * unit)
            merged[t, cb, 0] = total[rows, :lanes]
            merged[t, cb, 1] = total[rows, lanes:]
            place = tap * replicas + quarter * 2 + cb
            owner, local = place // 9, place % 9
            mine = owner == rep

            @pl.when(mine & outer)
            def _():
                merged_in[local, 0] = merged[t, cb, 0]

            @pl.when(mine & inner)
            def _():
                merged_in[local, 1] = merged[t, cb, 0]
                merged_in[local, 2] = merged[t, cb, 1]

            away = owner != rep
            start(away & outer, [functools.partial(merged_copy, t, cb, False, owner, local)])
            start(away & inner, [functools.partial(merged_copy, t, cb, True, owner, local)])

    for load in loads[4:]:
        load.wait()

    for local in range(9):
        place = rep * 9 + local
        of = (place % replicas) // 2
        its_half, its_y = of // 2, of % 2
        for wide, plane in ((False, 3 * its_half), (True, 1 + its_half)):
            @pl.when(index(plane, its_y) != rep)
            def _():
                merged_copy(0, 0, wide, rep, local).wait_recv()
        for tile in range(3):
            at = pl.ds(local * unit * 3 + tile, unit, stride=3)
            moved = 0.9 * momentum_v[at, :] + 0.0625 * merged_in[local, tile].astype(F32)
            new_momentum[at, :] = moved
            new_weights[at, :] = master_v[at, :] - 0.02 * moved

    for cond, copies in sent:
        if cond is None:
            for copy in copies:
                copy().wait_send()
        else:
            @pl.when(cond)
            def _():
                for copy in copies:
                    copy().wait_send()

    @pl.when(pipe > 0)
    def _():
        passing.wait_send()

    @pl.when(pipe < sections - 1)
    def _():
        passing.wait_recv()


def leave(passed, momentum, weights, passed_out, momentum_out, weights_out, sem):
    copies = [
        pltpu.make_async_copy(src, dst, sem.at[n])
        for n, (src, dst) in enumerate(
            ((momentum, momentum_out), (weights, weights_out), (passed, passed_out))
        )
    ]
    for copy in copies:
        copy.start()
    for copy in copies:
        copy.wait()


def factor_body(sections, replicas, activations, preactivation, upstream, weights, master, momentum):
    tile = activations.shape[3:]
    cols, channels = tile[1], tile[2]
    pixels = tile[0] * cols
    taps_rows = weights.shape[1]
    lanes = 128
    part, unit = channels // 4, channels // replicas
    flat = (momentum.shape[2] // lanes, lanes)
    big = pl.BlockSpec(memory_space=pl.ANY)
    here = pl.BlockSpec(memory_space=pltpu.VMEM)
    results = pl.pallas_call(
        functools.partial(kernel, sections, replicas, cols),
        out_shape=(
            pltpu.VMEM((pixels, channels), BF16),
            pltpu.VMEM(flat, F32),
            pltpu.VMEM(flat, F32),
        ),
        in_specs=[big] * 6,
        out_specs=(here,) * 3,
        scratch_shapes=[
            pltpu.VMEM((pixels, channels), BF16),
            pltpu.VMEM((pixels, channels), BF16),
            pltpu.VMEM((pixels, channels), BF16),
            pltpu.VMEM((taps_rows, channels), BF16),
            pltpu.VMEM((channels, pixels), BF16),
            pltpu.VMEM((pixels, channels), BF16),
            pltpu.VMEM((3, pixels, lanes), BF16),
            pltpu.VMEM((replicas, part, pixels), BF16),
            pltpu.VMEM((replicas, 2, pixels, lanes), BF16),
            pltpu.VMEM((replicas, 9 * part, pixels), BF16),
            pltpu.VMEM((replicas, 9 * part, 2 * lanes), F32),
            pltpu.VMEM((replicas, replicas, lanes), F32),
            pltpu.VMEM((replicas, replicas, lanes), F32),
            pltpu.VMEM((9, 2, 2, unit, lanes), BF16),
            pltpu.VMEM((9, 3, unit, lanes), BF16),
            pltpu.VMEM((3, pixels + 2 * cols, channels), BF16),
            pltpu.VMEM((pixels, channels), BF16),
            pltpu.SemaphoreType.DMA((6,)),
            pltpu.SemaphoreType.DMA((9,)),
            pltpu.SemaphoreType.DMA((replicas,)),
            pltpu.SemaphoreType.DMA((8, 2)),
            pltpu.SemaphoreType.DMA((replicas, 2)),
            pltpu.SemaphoreType.DMA((replicas,)),
            pltpu.SemaphoreType.DMA((replicas,)),
            pltpu.SemaphoreType.DMA((9, 2)),
            pltpu.SemaphoreType.DMA((9, 2)),
            pltpu.SemaphoreType.DMA((2,)),
            pltpu.VMEM(flat, F32),
            pltpu.VMEM(flat, F32),
        ],
        compiler_params=pltpu.CompilerParams(
            collective_id=0, has_side_effects=True, vmem_limit_bytes=56 * 1024 * 1024
        ),
    )(
        activations.reshape(pixels, channels),
        preactivation.reshape(pixels, channels),
        upstream.reshape(pixels, channels),
        weights[0],
        master.reshape(flat),
        momentum.reshape(flat),
    )
    passed, new_momentum, new_weights = results
    return (
        passed.reshape(activations.shape),
        new_momentum.reshape(momentum.shape),
        new_weights.reshape(master.shape),
    )


def pick(sections, replicas, *arrays):
    activations, weights, momentum = arrays[0], arrays[3], arrays[5]
    channels = activations.shape[5]
    fits = (
        replicas == 8
        and activations.shape[2] == 1
        and weights.shape[1] == 9 * channels
        and weights.shape[2] == channels
        and channels == 3 * 128
        and (activations.shape[3] * activations.shape[4]) % 128 == 0
        and activations.shape[4] % 16 == 0
        and momentum.shape[2] % 1024 == 0
    )
    return factor_body(sections, replicas, *arrays) if fits else body(*arrays)


def solution(mesh):
    return jax.shard_map(
        functools.partial(pick, mesh.shape["pipe"], mesh.shape["rep"]),
        mesh=mesh,
        in_specs=(
            P("pipe", "rep", None, None, None, None),
            P("pipe", "rep", None, None, None, None),
            P("pipe", "rep", None, None, None, None),
            P("pipe", None, None),
            P("pipe", "rep", None),
            P("pipe", "rep", None),
        ),
        out_specs=(
            P("pipe", "rep", None, None, None, None),
            P("pipe", "rep", None),
            P("pipe", "rep", None),
        ),
        check_vma=False,
    )
```

```python
import functools

import jax
import jax.numpy as jnp
from jax import lax
from jax.experimental import pallas as pl
from jax.experimental.pallas import tpu as pltpu
from jax.sharding import PartitionSpec as P

EPS = 1e-06


def swapped(shard, axis, stride):
    return lax.ppermute(shard, axis, [(i, i ^ 1 << stride) for i in range(lax.axis_size(axis))])


def from_behind(shard, axis, by):
    count = lax.axis_size(axis)
    pairs = [(i, i + by) for i in range(count) if 0 <= i + by < count]
    return lax.ppermute(shard, axis, pairs)


def shifted_patches(tile_data, flipped):
    frames, tile_rows, tile_cols, channels = tile_data.shape
    padded = jnp.pad(tile_data, ((0, 0), (1, 1), (1, 1), (0, 0)))
    if flipped:
        offsets = [(2 - row_off, 2 - col_off) for row_off in range(3) for col_off in range(3)]
    else:
        offsets = [(row_off, col_off) for row_off in range(3) for col_off in range(3)]
    pieces = [
        padded[:, first : first + tile_rows, second : second + tile_cols, :]
        for first, second in offsets
    ]
    return jnp.concatenate(pieces, axis=-1).reshape(frames * tile_rows * tile_cols, 9 * channels)


def local_backward(tile_data, preact_tile, upstream_tile, kernel):
    frames, tile_rows, tile_cols, channels = tile_data.shape
    pre_float = preact_tile.astype(jnp.float32)
    sigmoid_val = jax.nn.sigmoid(pre_float)
    local_grad = (
        upstream_tile.astype(jnp.float32) * sigmoid_val * (1.0 + pre_float * (1.0 - sigmoid_val))
    ).astype(jnp.bfloat16)
    flat_grad = local_grad.reshape(-1, channels)
    patches = shifted_patches(tile_data, False)
    weight_grad = lax.dot_general(
        patches, flat_grad, (((0,), (0,)), ((), ())), preferred_element_type=jnp.float32
    ).astype(jnp.bfloat16)
    grad_patches = shifted_patches(local_grad, True).reshape(-1, 9, channels)
    kernel_taps = kernel.reshape(9, channels, channels)
    summed = lax.dot_general(
        grad_patches, kernel_taps, (((1, 2), (0, 2)), ((), ())), preferred_element_type=jnp.float32
    )
    return (
        weight_grad,
        summed.astype(jnp.bfloat16).reshape(frames, tile_rows, tile_cols, channels),
    )


def group_sum(partials, sum_bits):
    for bit_number in range(sum_bits):
        partials = partials + swapped(partials, "rep", bit_number)
    return partials


def body(activations, preactivation, upstream, weights, master, momentum):
    weight_grad, input_grad = local_backward(
        activations[0, 0], preactivation[0, 0], upstream[0, 0], weights[0]
    )
    passed = from_behind(input_grad, "pipe", -1)
    replicas = lax.axis_size("rep")
    level_count = replicas.bit_length() - 1
    rep_index = lax.axis_index("rep")
    held_rows = weight_grad.reshape(replicas, -1)
    for level_num in range(level_count):
        is_lower = jnp.right_shift(rep_index, level_num) & 1 == 0
        paired = held_rows.reshape(-1, 2, held_rows.shape[1])
        keep_rows = jnp.where(is_lower, paired[:, 0], paired[:, 1])
        give_rows = jnp.where(is_lower, paired[:, 1], paired[:, 0])
        other_rows = swapped(give_rows, "rep", level_num)
        keep_float = keep_rows.astype(jnp.float32)
        other_float = other_rows.astype(jnp.float32)
        keep_sq = jnp.sum(keep_float * keep_float)
        other_sq = jnp.sum(other_float * other_float)
        partials = jnp.stack(
            [
                jnp.where(is_lower, keep_sq, other_sq),
                jnp.where(is_lower, other_sq, keep_sq),
                jnp.sum(keep_float * other_float),
            ]
        )
        sum_bits = level_num + 1
        partials = group_sum(partials, sum_bits)
        lower_coef = 1.0 - partials[2] / (2.0 * partials[0] + EPS)
        upper_coef = 1.0 - partials[2] / (2.0 * partials[1] + EPS)
        keep_coef = jnp.where(is_lower, lower_coef, upper_coef)
        other_coef = jnp.where(is_lower, upper_coef, lower_coef)
        merged = keep_coef * keep_rows.astype(jnp.float32) + other_coef * other_rows.astype(
            jnp.float32
        )
        held_rows = merged.astype(jnp.bfloat16)
    combined = held_rows.astype(jnp.float32).reshape(momentum.shape)
    new_momentum = 0.9 * momentum + 0.0625 * combined
    new_weights = master - 0.02 * new_momentum
    return (passed[None, None], new_momentum, new_weights)


MESH = pl.DeviceIdType.MESH
F32 = jnp.float32
BF16 = jnp.bfloat16


def fold(product):
    return jnp.sum(product.reshape(-1, 8, product.shape[-1]), axis=0)


def roles(z, y, rep):
    half = z // 2
    near = z + 1 - 2 * (z % 2)
    across = 2 - half
    far = 3 - 3 * half
    return half, near, across, far


def adasum_weights(gram):
    count = gram.shape[0]
    row = lax.broadcasted_iota(jnp.int32, gram.shape, 0)
    lane = lax.broadcasted_iota(jnp.int32, gram.shape, 1)
    weight = None
    bit = 1
    while bit < count:
        own = jnp.where(lane == row, gram, 0.0)
        cross = jnp.where(lane == row ^ bit, gram, 0.0)

        def coef(axis):
            sq = jnp.maximum(jnp.sum(own, axis=axis, keepdims=True), 0.0)
            return 1.0 - jnp.sum(cross, axis=axis, keepdims=True) / (2.0 * sq + EPS)

        down = coef(1)
        weight = down if weight is None else weight * down
        if 2 * bit < count:
            gram = down * gram * coef(0)
            gram = gram + jnp.where(
                row & bit == 0, pltpu.roll(gram, count - bit, 0), pltpu.roll(gram, bit, 0)
            )
            lanes = gram.shape[1]
            gram = gram + jnp.where(
                lane & bit == 0, pltpu.roll(gram, lanes - bit, 1), pltpu.roll(gram, bit, 1)
            )
        bit *= 2
    return weight


def kernel(
    sections, replicas, cols,
    act_hbm, pre_hbm, up_hbm, weights_hbm, master_hbm, momentum_hbm,
    passed_ref, combined_ref, master_v, momentum_v,
    act_v, pre_v, up_v, kernel_v, act_t, grad_v, grad_tiles,
    act_in, grad_in, patches, blocks, pair_sums, gram_in, merged, merged_in, shifted, igrad,
    load_sem, act_send, act_recv, grad_send, grad_recv, gram_send, gram_recv,
    merged_send, merged_recv, pass_sem,
):
    pixels, channels = act_v.shape
    part = channels // 4
    lanes = 128
    unit = channels // replicas
    pipe, rep = lax.axis_index("pipe"), lax.axis_index("rep")
    z, y = rep // 2, rep % 2
    half, near, across, far = roles(z, y, rep)
    outer = (z == 0) | (z == 3)
    inner = (z == 1) | (z == 2)
    quarter = half * 2 + y

    barrier = pltpu.get_barrier_semaphore()
    for step in range(1, replicas):
        peer = lax.rem(rep + step, replicas)
        pl.semaphore_signal(barrier, inc=1, device_id=(pipe, peer), device_id_type=MESH)

    @pl.when(pipe < sections - 1)
    def _():
        pl.semaphore_signal(barrier, inc=1, device_id=(pipe + 1, rep), device_id_type=MESH)

    loads = [
        pltpu.make_async_copy(src, dst, load_sem.at[n])
        for n, (src, dst) in enumerate(
            (
                (act_hbm, act_v), (pre_hbm, pre_v), (up_hbm, up_v), (weights_hbm, kernel_v),
                (master_hbm, master_v), (momentum_hbm, momentum_v),
            )
        )
    ]
    for load in loads:
        load.start()

    def index(zz, yy):
        return zz * 2 + yy

    def remote(src, dst, send, recv, target):
        return pltpu.make_async_remote_copy(
            src_ref=src, dst_ref=dst, send_sem=send, recv_sem=recv,
            device_id=(pipe, target), device_id_type=MESH,
        )

    def act_own(slot, block_of, target):
        rows = pl.ds(pl.multiple_of(block_of * part, part), part)
        return remote(act_t.at[rows, :], act_in.at[rep], act_send.at[slot], act_recv.at[rep], target)

    def act_pass(slot, block):
        return remote(
            act_in.at[block], act_in.at[block], act_send.at[slot], act_recv.at[block], index(near, y)
        )

    def grad_copy(slot, i, src, block, target):
        return remote(
            src, grad_in.at[block, i], grad_send.at[slot, i], grad_recv.at[block, i], target
        )

    other_inner = 2 - half
    own_acts = (
        (0, quarter, index(near, y)),
        (1, half * 2 + 1 - y, index(z, 1 - y)),
        (2, (1 - half) * 2 + y, index(other_inner, y)),
        (3, (1 - half) * 2 + 1 - y, index(other_inner, 1 - y)),
    )
    order = [
        index(z, y), index(z, 1 - y), index(near, y), index(across, y),
        index(near, 1 - y), index(across, 1 - y), index(far, y), index(far, 1 - y),
    ]

    sent = []

    def start(cond, copies):
        if cond is None:
            for copy in copies:
                copy().start()
        else:
            @pl.when(cond)
            def _():
                for copy in copies:
                    copy().start()
        sent.append((cond, copies))

    def wait_act(block):
        act_pass(4, block).wait_recv()

    def wait_grad(block):
        grad_copy(0, 0, grad_in.at[block, 0], block, rep).wait_recv()

        @pl.when(inner)
        def _():
            grad_copy(0, 1, grad_in.at[block, 1], block, rep).wait_recv()

    def own_grad(slot, tiles, target):
        return [
            functools.partial(grad_copy, slot, i, grad_tiles.at[tile], rep, target)
            for i, tile in enumerate(tiles)
        ]

    def pass_grad(slot, block, target, extra=None):
        start(None, [functools.partial(grad_copy, slot, 0, grad_in.at[block, 0], block, target)])
        start(inner, [functools.partial(grad_copy, slot, 1, grad_in.at[block, 1], block, target)])

    def patch(block):
        tile = act_in[block].astype(F32)
        pixel = lax.broadcasted_iota(jnp.int32, (1, pixels), 1)
        column = pixel % cols
        for j in range(3):
            if j == 1:
                moved = tile
            else:
                moved = pltpu.roll(tile, (1 - j) % pixels, 1)
                moved = jnp.where(column > 0 if j == 0 else column < cols - 1, moved, 0.0)
            for i in range(3):
                if i == 1:
                    placed = moved
                else:
                    placed = pltpu.roll(moved, ((1 - i) * cols) % pixels, 1)
                    placed = jnp.where(
                        pixel >= cols if i == 0 else pixel < pixels - cols, placed, 0.0
                    )
                patches[block, pl.ds((i * 3 + j) * part, part), :] = placed.astype(BF16)

    def multiply(k):
        block = order[k]
        grad = jnp.concatenate([grad_in[block, 0], grad_in[block, 1]], axis=1)

        for i in range(3):
            rows = pl.ds(3 * i * part, 3 * part)
            blocks[block, rows, :] = jnp.dot(
                patches[block, rows, :], grad, preferred_element_type=F32
            )

        def step(t, sums):
            here = pl.ds(pl.multiple_of(t * part, part), part)
            new = blocks[block, here, :]
            out = []
            for m in range(k + 1):
                against = new if m == k else blocks[order[m], here, :]
                folded = fold(new * against)
                out.append(sums[m] + folded[:, :lanes] + folded[:, lanes:])
            return tuple(out)

        zero = jnp.zeros((8, lanes), F32)
        sums = lax.fori_loop(0, 9, step, (zero,) * (k + 1), unroll=3)
        for m in range(k + 1):
            total = jnp.sum(sums[m], axis=0, keepdims=True)
            pair_sums[order[m], pl.ds(block, 1), :] = total
            if m < k:
                pair_sums[block, pl.ds(order[m], 1), :] = total

    loads[0].wait()
    act_t[...] = act_v[...].T
    loads[1].wait()
    loads[2].wait()
    z_f = pre_v[...].astype(F32)
    sig = jax.nn.sigmoid(z_f)
    grad = (up_v[...].astype(F32) * sig * (1.0 + z_f * (1.0 - sig))).astype(BF16)
    grad_v[...] = grad
    for tile in range(3):
        grad_tiles[tile] = grad[:, tile * lanes : (tile + 1) * lanes]
    pl.semaphore_wait(barrier, replicas - 1 + (pipe > 0).astype(jnp.int32))
    start(None, [functools.partial(act_own, *args) for args in own_acts])
    start(inner, own_grad(1, (1, 2), index(across, y)))
    start(outer, own_grad(1, (1, 2), index(near, y)))
    start(inner, own_grad(0, (1, 2), index(z, 1 - y)))
    start(outer, own_grad(0, (0,), index(z, 1 - y)))
    start(outer, own_grad(2, (0,), index(far, y)))
    start(inner, own_grad(2, (0,), index(near, y)))
    start(inner, own_grad(3, (0,), index(far, y)))

    act_in[rep] = act_t[pl.ds(pl.multiple_of(quarter * part, part), part), :]

    @pl.when(outer)
    def _():
        grad_in[rep, 0] = grad_tiles[0]
        for block in range(replicas):
            grad_in[block, 1] = jnp.zeros((pixels, lanes), BF16)

    @pl.when(inner)
    def _():
        grad_in[rep, 0] = grad_tiles[1]
        grad_in[rep, 1] = grad_tiles[2]

    def relay(slot, k):
        @pl.when(inner)
        def _():
            wait_act(order[k])

        start(inner, [functools.partial(act_pass, slot, order[k])])

    def take(k, relayed):
        if relayed:
            @pl.when(outer)
            def _():
                wait_act(order[k])
        else:
            wait_act(order[k])
        patch(order[k])

    patch(rep)
    multiply(0)
    wait_act(order[1])
    start(None, [functools.partial(act_pass, 4, order[1])])
    relay(5, 3)
    relay(6, 5)
    patch(order[1])
    wait_grad(order[2])
    pass_grad(4, order[2], index(z, 1 - y))
    start(inner, [
        functools.partial(grad_copy, 5, i, grad_in.at[order[2], i], order[2], index(across, y))
        for i in range(2)
    ])
    relay(7, 6)
    relay(8, 7)
    wait_grad(order[1])
    multiply(1)
    wait_grad(order[3])
    pass_grad(6, order[3], index(z, 1 - y))
    take(2, False)
    multiply(2)
    take(3, True)
    multiply(3)
    wait_grad(order[6])
    pass_grad(7, order[6], index(z, 1 - y))
    take(4, False)
    take(5, True)
    wait_grad(order[4])
    multiply(4)
    wait_grad(order[5])
    multiply(5)
    take(6, True)
    multiply(6)
    take(7, True)
    wait_grad(order[7])
    multiply(7)

    lane = lax.broadcasted_iota(jnp.int32, (replicas, lanes), 1)
    gram = jnp.zeros((replicas, lanes), F32)
    for block in range(replicas):
        gram = jnp.where(lane == block, jnp.sum(pair_sums[block], axis=1, keepdims=True), gram)
    gram_in[rep] = gram

    def gram_copy(step):
        peer = lax.rem(rep + step, replicas)
        return remote(gram_in.at[rep], gram_in.at[rep], gram_send.at[step], gram_recv.at[rep], peer)

    def gram_from(step):
        peer = lax.rem(rep + step, replicas)
        return remote(gram_in.at[peer], gram_in.at[peer], gram_send.at[step], gram_recv.at[peer], peer)

    for step in range(1, replicas):
        start(None, [functools.partial(gram_copy, step)])

    edge = jnp.zeros((cols, channels), BF16)
    for j in range(3):
        shifted[j, pl.ds(0, cols), :] = edge
        shifted[j, pl.ds(cols + pixels, cols), :] = edge
    grad = grad_v[...].astype(F32)
    column = lax.broadcasted_iota(jnp.int32, (pixels, channels), 0) % cols
    here = pl.ds(cols, pixels)
    shifted[0, here, :] = jnp.where(column < cols - 1, pltpu.roll(grad, pixels - 1, 0), 0.0).astype(BF16)
    shifted[1, here, :] = grad_v[...]
    shifted[2, here, :] = jnp.where(column > 0, pltpu.roll(grad, 1, 0), 0.0).astype(BF16)
    loads[3].wait()
    total = jnp.zeros((pixels, channels), F32)
    for i in range(3):
        for j in range(3):
            total = total + lax.dot_general(
                shifted[j, pl.ds((2 - i) * cols, pixels), :],
                kernel_v[pl.ds((i * 3 + j) * channels, channels), :],
                (((1,), (1,)), ((), ())),
                preferred_element_type=F32,
            )
    igrad[...] = total.astype(BF16)

    @pl.when(pipe == sections - 1)
    def _():
        passed_ref[...] = jnp.zeros_like(passed_ref)

    passing = pltpu.make_async_remote_copy(
        src_ref=igrad,
        dst_ref=passed_ref,
        send_sem=pass_sem.at[0],
        recv_sem=pass_sem.at[1],
        device_id=(jnp.maximum(pipe - 1, 0), rep),
        device_id_type=MESH,
    )

    @pl.when(pipe > 0)
    def _():
        passing.start()

    for step in range(1, replicas):
        gram_from(step).wait_recv()
    gram = gram_in[0]
    for block in range(1, replicas):
        gram = gram + gram_in[block]
    weight = adasum_weights(gram)

    def merged_copy(t, cb, wide, owner, local):
        src = merged.at[t, cb] if wide else merged.at[t, cb, pl.ds(0, 1)]
        dst = merged_in.at[local, pl.ds(1, 2)] if wide else merged_in.at[local, pl.ds(0, 1)]
        kind = 1 if wide else 0
        return remote(src, dst, merged_send.at[t, cb], merged_recv.at[local, kind], owner)

    for t in range(9):
        tap = t + (1 - half) * (8 - 2 * t)
        here = pl.ds(pl.multiple_of(tap * part, part), part)
        total = weight[0:1, 0:1] * blocks[0, here, :]
        for block in range(1, replicas):
            total = total + weight[block : block + 1, 0:1] * blocks[block, here, :]
        total = total.astype(BF16)
        for cb in range(2):
            rows = slice(cb * unit, (cb + 1) * unit)
            merged[t, cb, 0] = total[rows, :lanes]
            merged[t, cb, 1] = total[rows, lanes:]
            place = tap * replicas + quarter * 2 + cb
            owner, local = place // 9, place % 9
            mine = owner == rep

            @pl.when(mine & outer)
            def _():
                merged_in[local, 0] = merged[t, cb, 0]

            @pl.when(mine & inner)
            def _():
                merged_in[local, 1] = merged[t, cb, 0]
                merged_in[local, 2] = merged[t, cb, 1]

            away = owner != rep
            start(away & outer, [functools.partial(merged_copy, t, cb, False, owner, local)])
            start(away & inner, [functools.partial(merged_copy, t, cb, True, owner, local)])

    for load in loads[4:]:
        load.wait()

    for local in range(9):
        place = rep * 9 + local
        of = (place % replicas) // 2
        its_half, its_y = of // 2, of % 2
        for wide, plane in ((False, 3 * its_half), (True, 1 + its_half)):
            @pl.when(index(plane, its_y) != rep)
            def _():
                merged_copy(0, 0, wide, rep, local).wait_recv()
        for tile in range(3):
            at = pl.ds(local * unit * 3 + tile, unit, stride=3)
            combined_ref[at, :] = merged_in[local, tile].astype(F32)

    for cond, copies in sent:
        if cond is None:
            for copy in copies:
                copy().wait_send()
        else:
            @pl.when(cond)
            def _():
                for copy in copies:
                    copy().wait_send()

    @pl.when(pipe > 0)
    def _():
        passing.wait_send()

    @pl.when(pipe < sections - 1)
    def _():
        passing.wait_recv()


def leave(passed, momentum, weights, passed_out, momentum_out, weights_out, sem):
    copies = [
        pltpu.make_async_copy(src, dst, sem.at[n])
        for n, (src, dst) in enumerate(
            ((momentum, momentum_out), (weights, weights_out), (passed, passed_out))
        )
    ]
    for copy in copies:
        copy.start()
    for copy in copies:
        copy.wait()


def factor_body(sections, replicas, activations, preactivation, upstream, weights, master, momentum):
    tile = activations.shape[3:]
    cols, channels = tile[1], tile[2]
    pixels = tile[0] * cols
    taps_rows = weights.shape[1]
    lanes = 128
    part, unit = channels // 4, channels // replicas
    owned = momentum.shape
    flat = (owned[2] // lanes, lanes)
    big = pl.BlockSpec(memory_space=pl.ANY)
    here = pl.BlockSpec(memory_space=pltpu.VMEM)
    passed, combined, master, momentum = pl.pallas_call(
        functools.partial(kernel, sections, replicas, cols),
        out_shape=(
            pltpu.VMEM((pixels, channels), BF16),
            pltpu.VMEM(flat, F32),
            pltpu.VMEM(flat, F32),
            pltpu.VMEM(flat, F32),
        ),
        in_specs=[big] * 6,
        out_specs=(here,) * 4,
        scratch_shapes=[
            pltpu.VMEM((pixels, channels), BF16),
            pltpu.VMEM((pixels, channels), BF16),
            pltpu.VMEM((pixels, channels), BF16),
            pltpu.VMEM((taps_rows, channels), BF16),
            pltpu.VMEM((channels, pixels), BF16),
            pltpu.VMEM((pixels, channels), BF16),
            pltpu.VMEM((3, pixels, lanes), BF16),
            pltpu.VMEM((replicas, part, pixels), BF16),
            pltpu.VMEM((replicas, 2, pixels, lanes), BF16),
            pltpu.VMEM((replicas, 9 * part, pixels), BF16),
            pltpu.VMEM((replicas, 9 * part, 2 * lanes), F32),
            pltpu.VMEM((replicas, replicas, lanes), F32),
            pltpu.VMEM((replicas, replicas, lanes), F32),
            pltpu.VMEM((9, 2, 2, unit, lanes), BF16),
            pltpu.VMEM((9, 3, unit, lanes), BF16),
            pltpu.VMEM((3, pixels + 2 * cols, channels), BF16),
            pltpu.VMEM((pixels, channels), BF16),
            pltpu.SemaphoreType.DMA((6,)),
            pltpu.SemaphoreType.DMA((9,)),
            pltpu.SemaphoreType.DMA((replicas,)),
            pltpu.SemaphoreType.DMA((8, 2)),
            pltpu.SemaphoreType.DMA((replicas, 2)),
            pltpu.SemaphoreType.DMA((replicas,)),
            pltpu.SemaphoreType.DMA((replicas,)),
            pltpu.SemaphoreType.DMA((9, 2)),
            pltpu.SemaphoreType.DMA((9, 2)),
            pltpu.SemaphoreType.DMA((2,)),
        ],
        compiler_params=pltpu.CompilerParams(
            collective_id=0, has_side_effects=True, vmem_limit_bytes=56 * 1024 * 1024
        ),
    )(
        activations.reshape(pixels, channels),
        preactivation.reshape(pixels, channels),
        upstream.reshape(pixels, channels),
        weights[0],
        master.reshape(flat),
        momentum.reshape(flat),
    )
    new_momentum = 0.9 * momentum + 0.0625 * combined
    new_weights = master - 0.02 * new_momentum
    return (
        passed.reshape(activations.shape),
        new_momentum.reshape(owned),
        new_weights.reshape(owned),
    )


def pick(sections, replicas, *arrays):
    activations, weights, momentum = arrays[0], arrays[3], arrays[5]
    channels = activations.shape[5]
    fits = (
        replicas == 8
        and activations.shape[2] == 1
        and weights.shape[1] == 9 * channels
        and weights.shape[2] == channels
        and channels == 3 * 128
        and (activations.shape[3] * activations.shape[4]) % 128 == 0
        and activations.shape[4] % 16 == 0
        and momentum.shape[2] % 1024 == 0
    )
    return factor_body(sections, replicas, *arrays) if fits else body(*arrays)


def solution(mesh):
    return jax.shard_map(
        functools.partial(pick, mesh.shape["pipe"], mesh.shape["rep"]),
        mesh=mesh,
        in_specs=(
            P("pipe", "rep", None, None, None, None),
            P("pipe", "rep", None, None, None, None),
            P("pipe", "rep", None, None, None, None),
            P("pipe", None, None),
            P("pipe", "rep", None),
            P("pipe", "rep", None),
        ),
        out_specs=(
            P("pipe", "rep", None, None, None, None),
            P("pipe", "rep", None),
            P("pipe", "rep", None),
        ),
        check_vma=False,
    )
```

```python
import functools

import jax
import jax.numpy as jnp
from jax import lax
from jax.experimental import pallas as pl
from jax.experimental.pallas import tpu as pltpu
from jax.sharding import PartitionSpec as P

EPS = 1e-06


def swapped(shard, axis, stride):
    return lax.ppermute(shard, axis, [(i, i ^ 1 << stride) for i in range(lax.axis_size(axis))])


def from_behind(shard, axis, by):
    count = lax.axis_size(axis)
    pairs = [(i, i + by) for i in range(count) if 0 <= i + by < count]
    return lax.ppermute(shard, axis, pairs)


def shifted_patches(tile_data, flipped):
    frames, tile_rows, tile_cols, channels = tile_data.shape
    padded = jnp.pad(tile_data, ((0, 0), (1, 1), (1, 1), (0, 0)))
    if flipped:
        offsets = [(2 - row_off, 2 - col_off) for row_off in range(3) for col_off in range(3)]
    else:
        offsets = [(row_off, col_off) for row_off in range(3) for col_off in range(3)]
    pieces = [
        padded[:, first : first + tile_rows, second : second + tile_cols, :]
        for first, second in offsets
    ]
    return jnp.concatenate(pieces, axis=-1).reshape(frames * tile_rows * tile_cols, 9 * channels)


def local_backward(tile_data, preact_tile, upstream_tile, kernel):
    frames, tile_rows, tile_cols, channels = tile_data.shape
    pre_float = preact_tile.astype(jnp.float32)
    sigmoid_val = jax.nn.sigmoid(pre_float)
    local_grad = (
        upstream_tile.astype(jnp.float32) * sigmoid_val * (1.0 + pre_float * (1.0 - sigmoid_val))
    ).astype(jnp.bfloat16)
    flat_grad = local_grad.reshape(-1, channels)
    patches = shifted_patches(tile_data, False)
    weight_grad = lax.dot_general(
        patches, flat_grad, (((0,), (0,)), ((), ())), preferred_element_type=jnp.float32
    ).astype(jnp.bfloat16)
    grad_patches = shifted_patches(local_grad, True).reshape(-1, 9, channels)
    kernel_taps = kernel.reshape(9, channels, channels)
    summed = lax.dot_general(
        grad_patches, kernel_taps, (((1, 2), (0, 2)), ((), ())), preferred_element_type=jnp.float32
    )
    return (
        weight_grad,
        summed.astype(jnp.bfloat16).reshape(frames, tile_rows, tile_cols, channels),
    )


def group_sum(partials, sum_bits):
    for bit_number in range(sum_bits):
        partials = partials + swapped(partials, "rep", bit_number)
    return partials


def body(activations, preactivation, upstream, weights, master, momentum):
    weight_grad, input_grad = local_backward(
        activations[0, 0], preactivation[0, 0], upstream[0, 0], weights[0]
    )
    passed = from_behind(input_grad, "pipe", -1)
    replicas = lax.axis_size("rep")
    level_count = replicas.bit_length() - 1
    rep_index = lax.axis_index("rep")
    held_rows = weight_grad.reshape(replicas, -1)
    for level_num in range(level_count):
        is_lower = jnp.right_shift(rep_index, level_num) & 1 == 0
        paired = held_rows.reshape(-1, 2, held_rows.shape[1])
        keep_rows = jnp.where(is_lower, paired[:, 0], paired[:, 1])
        give_rows = jnp.where(is_lower, paired[:, 1], paired[:, 0])
        other_rows = swapped(give_rows, "rep", level_num)
        keep_float = keep_rows.astype(jnp.float32)
        other_float = other_rows.astype(jnp.float32)
        keep_sq = jnp.sum(keep_float * keep_float)
        other_sq = jnp.sum(other_float * other_float)
        partials = jnp.stack(
            [
                jnp.where(is_lower, keep_sq, other_sq),
                jnp.where(is_lower, other_sq, keep_sq),
                jnp.sum(keep_float * other_float),
            ]
        )
        sum_bits = level_num + 1
        partials = group_sum(partials, sum_bits)
        lower_coef = 1.0 - partials[2] / (2.0 * partials[0] + EPS)
        upper_coef = 1.0 - partials[2] / (2.0 * partials[1] + EPS)
        keep_coef = jnp.where(is_lower, lower_coef, upper_coef)
        other_coef = jnp.where(is_lower, upper_coef, lower_coef)
        merged = keep_coef * keep_rows.astype(jnp.float32) + other_coef * other_rows.astype(
            jnp.float32
        )
        held_rows = merged.astype(jnp.bfloat16)
    combined = held_rows.astype(jnp.float32).reshape(momentum.shape)
    new_momentum = 0.9 * momentum + 0.0625 * combined
    new_weights = master - 0.02 * new_momentum
    return (passed[None, None], new_momentum, new_weights)


MESH = pl.DeviceIdType.MESH
F32 = jnp.float32
BF16 = jnp.bfloat16


def fold(product):
    return jnp.sum(product.reshape(-1, 8, product.shape[-1]), axis=0)


def roles(z, y, rep):
    half = z // 2
    near = z + 1 - 2 * (z % 2)
    across = 2 - half
    far = 3 - 3 * half
    return half, near, across, far


def adasum_weights(gram):
    count = gram.shape[0]
    row = lax.broadcasted_iota(jnp.int32, gram.shape, 0)
    lane = lax.broadcasted_iota(jnp.int32, gram.shape, 1)
    weight = None
    bit = 1
    while bit < count:
        own = jnp.where(lane == row, gram, 0.0)
        cross = jnp.where(lane == row ^ bit, gram, 0.0)

        def coef(axis):
            sq = jnp.maximum(jnp.sum(own, axis=axis, keepdims=True), 0.0)
            return 1.0 - jnp.sum(cross, axis=axis, keepdims=True) / (2.0 * sq + EPS)

        down = coef(1)
        weight = down if weight is None else weight * down
        if 2 * bit < count:
            gram = down * gram * coef(0)
            gram = gram + jnp.where(
                row & bit == 0, pltpu.roll(gram, count - bit, 0), pltpu.roll(gram, bit, 0)
            )
            lanes = gram.shape[1]
            gram = gram + jnp.where(
                lane & bit == 0, pltpu.roll(gram, lanes - bit, 1), pltpu.roll(gram, bit, 1)
            )
        bit *= 2
    return weight


def kernel(
    sections, replicas, cols,
    act_hbm, pre_hbm, up_hbm, weights_hbm, master_hbm, momentum_hbm,
    passed_ref, combined_ref, master_v, momentum_v,
    act_v, pre_v, up_v, kernel_v, act_t, grad_v, grad_tiles,
    act_in, grad_in, patches, blocks, pair_sums, gram_in, merged, merged_in, shifted, igrad,
    load_sem, act_send, act_recv, grad_send, grad_recv, gram_send, gram_recv,
    merged_send, merged_recv, pass_sem,
):
    pixels, channels = act_v.shape
    part = channels // 4
    lanes = 128
    unit = channels // replicas
    pipe, rep = lax.axis_index("pipe"), lax.axis_index("rep")
    z, y = rep // 2, rep % 2
    half, near, across, far = roles(z, y, rep)
    outer = (z == 0) | (z == 3)
    inner = (z == 1) | (z == 2)
    quarter = half * 2 + y

    barrier = pltpu.get_barrier_semaphore()
    for step in range(1, replicas):
        peer = lax.rem(rep + step, replicas)
        pl.semaphore_signal(barrier, inc=1, device_id=(pipe, peer), device_id_type=MESH)

    @pl.when(pipe < sections - 1)
    def _():
        pl.semaphore_signal(barrier, inc=1, device_id=(pipe + 1, rep), device_id_type=MESH)

    loads = [
        pltpu.make_async_copy(src, dst, load_sem.at[n])
        for n, (src, dst) in enumerate(
            (
                (act_hbm, act_v), (pre_hbm, pre_v), (up_hbm, up_v), (weights_hbm, kernel_v),
                (master_hbm, master_v), (momentum_hbm, momentum_v),
            )
        )
    ]
    for load in loads[:3]:
        load.start()

    def index(zz, yy):
        return zz * 2 + yy

    def remote(src, dst, send, recv, target):
        return pltpu.make_async_remote_copy(
            src_ref=src, dst_ref=dst, send_sem=send, recv_sem=recv,
            device_id=(pipe, target), device_id_type=MESH,
        )

    def act_own(slot, block_of, target):
        rows = pl.ds(pl.multiple_of(block_of * part, part), part)
        return remote(act_t.at[rows, :], act_in.at[rep], act_send.at[slot], act_recv.at[rep], target)

    def act_pass(slot, block):
        return remote(
            act_in.at[block], act_in.at[block], act_send.at[slot], act_recv.at[block], index(near, y)
        )

    def grad_copy(slot, i, src, block, target):
        return remote(
            src, grad_in.at[block, i], grad_send.at[slot, i], grad_recv.at[block, i], target
        )

    other_inner = 2 - half
    own_acts = (
        (0, quarter, index(near, y)),
        (1, half * 2 + 1 - y, index(z, 1 - y)),
        (2, (1 - half) * 2 + y, index(other_inner, y)),
        (3, (1 - half) * 2 + 1 - y, index(other_inner, 1 - y)),
    )
    order = [
        index(z, y), index(z, 1 - y), index(near, y), index(across, y),
        index(near, 1 - y), index(across, 1 - y), index(far, y), index(far, 1 - y),
    ]

    sent = []

    def start(cond, copies):
        if cond is None:
            for copy in copies:
                copy().start()
        else:
            @pl.when(cond)
            def _():
                for copy in copies:
                    copy().start()
        sent.append((cond, copies))

    def wait_act(block):
        act_pass(4, block).wait_recv()

    def wait_grad(block):
        grad_copy(0, 0, grad_in.at[block, 0], block, rep).wait_recv()

        @pl.when(inner)
        def _():
            grad_copy(0, 1, grad_in.at[block, 1], block, rep).wait_recv()

    def own_grad(slot, tiles, target):
        return [
            functools.partial(grad_copy, slot, i, grad_tiles.at[tile], rep, target)
            for i, tile in enumerate(tiles)
        ]

    def pass_grad(slot, block, target, extra=None):
        start(None, [functools.partial(grad_copy, slot, 0, grad_in.at[block, 0], block, target)])
        start(inner, [functools.partial(grad_copy, slot, 1, grad_in.at[block, 1], block, target)])

    def patch(block):
        tile = act_in[block].astype(F32)
        pixel = lax.broadcasted_iota(jnp.int32, (1, pixels), 1)
        column = pixel % cols
        for j in range(3):
            if j == 1:
                moved = tile
            else:
                moved = pltpu.roll(tile, (1 - j) % pixels, 1)
                moved = jnp.where(column > 0 if j == 0 else column < cols - 1, moved, 0.0)
            for i in range(3):
                if i == 1:
                    placed = moved
                else:
                    placed = pltpu.roll(moved, ((1 - i) * cols) % pixels, 1)
                    placed = jnp.where(
                        pixel >= cols if i == 0 else pixel < pixels - cols, placed, 0.0
                    )
                patches[block, pl.ds((i * 3 + j) * part, part), :] = placed.astype(BF16)

    def multiply(k):
        block = order[k]
        grad = jnp.concatenate([grad_in[block, 0], grad_in[block, 1]], axis=1)

        for i in range(3):
            rows = pl.ds(3 * i * part, 3 * part)
            blocks[block, rows, :] = jnp.dot(
                patches[block, rows, :], grad, preferred_element_type=F32
            )

        def step(t, sums):
            here = pl.ds(pl.multiple_of(t * part, part), part)
            new = blocks[block, here, :]
            out = []
            for m in range(k + 1):
                against = new if m == k else blocks[order[m], here, :]
                folded = fold(new * against)
                out.append(sums[m] + folded[:, :lanes] + folded[:, lanes:])
            return tuple(out)

        zero = jnp.zeros((8, lanes), F32)
        sums = lax.fori_loop(0, 9, step, (zero,) * (k + 1), unroll=3)
        for m in range(k + 1):
            total = jnp.sum(sums[m], axis=0, keepdims=True)
            pair_sums[order[m], pl.ds(block, 1), :] = total
            if m < k:
                pair_sums[block, pl.ds(order[m], 1), :] = total

    loads[0].wait()
    act_t[...] = act_v[...].T
    loads[1].wait()
    loads[2].wait()
    z_f = pre_v[...].astype(F32)
    sig = jax.nn.sigmoid(z_f)
    grad = (up_v[...].astype(F32) * sig * (1.0 + z_f * (1.0 - sig))).astype(BF16)
    for load in loads[3:]:
        load.start()
    grad_v[...] = grad
    for tile in range(3):
        grad_tiles[tile] = grad[:, tile * lanes : (tile + 1) * lanes]
    pl.semaphore_wait(barrier, replicas - 1 + (pipe > 0).astype(jnp.int32))
    start(None, [functools.partial(act_own, *args) for args in own_acts])
    start(inner, own_grad(1, (1, 2), index(across, y)))
    start(outer, own_grad(1, (1, 2), index(near, y)))
    start(inner, own_grad(0, (1, 2), index(z, 1 - y)))
    start(outer, own_grad(0, (0,), index(z, 1 - y)))
    start(outer, own_grad(2, (0,), index(far, y)))
    start(inner, own_grad(2, (0,), index(near, y)))
    start(inner, own_grad(3, (0,), index(far, y)))

    act_in[rep] = act_t[pl.ds(pl.multiple_of(quarter * part, part), part), :]

    @pl.when(outer)
    def _():
        grad_in[rep, 0] = grad_tiles[0]
        for block in range(replicas):
            grad_in[block, 1] = jnp.zeros((pixels, lanes), BF16)

    @pl.when(inner)
    def _():
        grad_in[rep, 0] = grad_tiles[1]
        grad_in[rep, 1] = grad_tiles[2]

    def relay(slot, k):
        @pl.when(inner)
        def _():
            wait_act(order[k])

        start(inner, [functools.partial(act_pass, slot, order[k])])

    def take(k, relayed):
        if relayed:
            @pl.when(outer)
            def _():
                wait_act(order[k])
        else:
            wait_act(order[k])
        patch(order[k])

    patch(rep)
    multiply(0)
    wait_act(order[1])
    start(None, [functools.partial(act_pass, 4, order[1])])
    relay(5, 3)
    relay(6, 5)
    patch(order[1])
    wait_grad(order[2])
    pass_grad(4, order[2], index(z, 1 - y))
    start(inner, [
        functools.partial(grad_copy, 5, i, grad_in.at[order[2], i], order[2], index(across, y))
        for i in range(2)
    ])
    relay(7, 6)
    relay(8, 7)
    wait_grad(order[1])
    multiply(1)
    wait_grad(order[3])
    pass_grad(6, order[3], index(z, 1 - y))
    take(2, False)
    multiply(2)
    take(3, True)
    multiply(3)
    wait_grad(order[6])
    pass_grad(7, order[6], index(z, 1 - y))
    take(4, False)
    take(5, True)
    wait_grad(order[4])
    multiply(4)
    wait_grad(order[5])
    multiply(5)
    take(6, True)
    multiply(6)
    take(7, True)
    wait_grad(order[7])
    multiply(7)

    lane = lax.broadcasted_iota(jnp.int32, (replicas, lanes), 1)
    gram = jnp.zeros((replicas, lanes), F32)
    for block in range(replicas):
        gram = jnp.where(lane == block, jnp.sum(pair_sums[block], axis=1, keepdims=True), gram)
    gram_in[rep] = gram

    def gram_copy(step):
        peer = lax.rem(rep + step, replicas)
        return remote(gram_in.at[rep], gram_in.at[rep], gram_send.at[step], gram_recv.at[rep], peer)

    def gram_from(step):
        peer = lax.rem(rep + step, replicas)
        return remote(gram_in.at[peer], gram_in.at[peer], gram_send.at[step], gram_recv.at[peer], peer)

    for step in range(1, replicas):
        start(None, [functools.partial(gram_copy, step)])

    edge = jnp.zeros((cols, channels), BF16)
    for j in range(3):
        shifted[j, pl.ds(0, cols), :] = edge
        shifted[j, pl.ds(cols + pixels, cols), :] = edge
    grad = grad_v[...].astype(F32)
    column = lax.broadcasted_iota(jnp.int32, (pixels, channels), 0) % cols
    here = pl.ds(cols, pixels)
    shifted[0, here, :] = jnp.where(column < cols - 1, pltpu.roll(grad, pixels - 1, 0), 0.0).astype(BF16)
    shifted[1, here, :] = grad_v[...]
    shifted[2, here, :] = jnp.where(column > 0, pltpu.roll(grad, 1, 0), 0.0).astype(BF16)
    loads[3].wait()
    total = jnp.zeros((pixels, channels), F32)
    for i in range(3):
        for j in range(3):
            total = total + lax.dot_general(
                shifted[j, pl.ds((2 - i) * cols, pixels), :],
                kernel_v[pl.ds((i * 3 + j) * channels, channels), :],
                (((1,), (1,)), ((), ())),
                preferred_element_type=F32,
            )
    igrad[...] = total.astype(BF16)

    @pl.when(pipe == sections - 1)
    def _():
        passed_ref[...] = jnp.zeros_like(passed_ref)

    passing = pltpu.make_async_remote_copy(
        src_ref=igrad,
        dst_ref=passed_ref,
        send_sem=pass_sem.at[0],
        recv_sem=pass_sem.at[1],
        device_id=(jnp.maximum(pipe - 1, 0), rep),
        device_id_type=MESH,
    )

    @pl.when(pipe > 0)
    def _():
        passing.start()

    for step in range(1, replicas):
        gram_from(step).wait_recv()
    gram = gram_in[0]
    for block in range(1, replicas):
        gram = gram + gram_in[block]
    weight = adasum_weights(gram)

    def merged_copy(t, cb, wide, owner, local):
        src = merged.at[t, cb] if wide else merged.at[t, cb, pl.ds(0, 1)]
        dst = merged_in.at[local, pl.ds(1, 2)] if wide else merged_in.at[local, pl.ds(0, 1)]
        kind = 1 if wide else 0
        return remote(src, dst, merged_send.at[t, cb], merged_recv.at[local, kind], owner)

    for t in range(9):
        tap = t + (1 - half) * (8 - 2 * t)
        here = pl.ds(pl.multiple_of(tap * part, part), part)
        total = weight[0:1, 0:1] * blocks[0, here, :]
        for block in range(1, replicas):
            total = total + weight[block : block + 1, 0:1] * blocks[block, here, :]
        total = total.astype(BF16)
        for cb in range(2):
            rows = slice(cb * unit, (cb + 1) * unit)
            merged[t, cb, 0] = total[rows, :lanes]
            merged[t, cb, 1] = total[rows, lanes:]
            place = tap * replicas + quarter * 2 + cb
            owner, local = place // 9, place % 9
            mine = owner == rep

            @pl.when(mine & outer)
            def _():
                merged_in[local, 0] = merged[t, cb, 0]

            @pl.when(mine & inner)
            def _():
                merged_in[local, 1] = merged[t, cb, 0]
                merged_in[local, 2] = merged[t, cb, 1]

            away = owner != rep
            start(away & outer, [functools.partial(merged_copy, t, cb, False, owner, local)])
            start(away & inner, [functools.partial(merged_copy, t, cb, True, owner, local)])

    for load in loads[4:]:
        load.wait()

    for local in range(9):
        place = rep * 9 + local
        of = (place % replicas) // 2
        its_half, its_y = of // 2, of % 2
        for wide, plane in ((False, 3 * its_half), (True, 1 + its_half)):
            @pl.when(index(plane, its_y) != rep)
            def _():
                merged_copy(0, 0, wide, rep, local).wait_recv()
        for tile in range(3):
            at = pl.ds(local * unit * 3 + tile, unit, stride=3)
            combined_ref[at, :] = merged_in[local, tile].astype(F32)

    for cond, copies in sent:
        if cond is None:
            for copy in copies:
                copy().wait_send()
        else:
            @pl.when(cond)
            def _():
                for copy in copies:
                    copy().wait_send()

    @pl.when(pipe > 0)
    def _():
        passing.wait_send()

    @pl.when(pipe < sections - 1)
    def _():
        passing.wait_recv()


def leave(passed, momentum, weights, passed_out, momentum_out, weights_out, sem):
    copies = [
        pltpu.make_async_copy(src, dst, sem.at[n])
        for n, (src, dst) in enumerate(
            ((momentum, momentum_out), (weights, weights_out), (passed, passed_out))
        )
    ]
    for copy in copies:
        copy.start()
    for copy in copies:
        copy.wait()


def factor_body(sections, replicas, activations, preactivation, upstream, weights, master, momentum):
    tile = activations.shape[3:]
    cols, channels = tile[1], tile[2]
    pixels = tile[0] * cols
    taps_rows = weights.shape[1]
    lanes = 128
    part, unit = channels // 4, channels // replicas
    owned = momentum.shape
    flat = (owned[2] // lanes, lanes)
    big = pl.BlockSpec(memory_space=pl.ANY)
    here = pl.BlockSpec(memory_space=pltpu.VMEM)
    passed, combined, master, momentum = pl.pallas_call(
        functools.partial(kernel, sections, replicas, cols),
        out_shape=(
            pltpu.VMEM((pixels, channels), BF16),
            pltpu.VMEM(flat, F32),
            pltpu.VMEM(flat, F32),
            pltpu.VMEM(flat, F32),
        ),
        in_specs=[big] * 6,
        out_specs=(here,) * 4,
        scratch_shapes=[
            pltpu.VMEM((pixels, channels), BF16),
            pltpu.VMEM((pixels, channels), BF16),
            pltpu.VMEM((pixels, channels), BF16),
            pltpu.VMEM((taps_rows, channels), BF16),
            pltpu.VMEM((channels, pixels), BF16),
            pltpu.VMEM((pixels, channels), BF16),
            pltpu.VMEM((3, pixels, lanes), BF16),
            pltpu.VMEM((replicas, part, pixels), BF16),
            pltpu.VMEM((replicas, 2, pixels, lanes), BF16),
            pltpu.VMEM((replicas, 9 * part, pixels), BF16),
            pltpu.VMEM((replicas, 9 * part, 2 * lanes), F32),
            pltpu.VMEM((replicas, replicas, lanes), F32),
            pltpu.VMEM((replicas, replicas, lanes), F32),
            pltpu.VMEM((9, 2, 2, unit, lanes), BF16),
            pltpu.VMEM((9, 3, unit, lanes), BF16),
            pltpu.VMEM((3, pixels + 2 * cols, channels), BF16),
            pltpu.VMEM((pixels, channels), BF16),
            pltpu.SemaphoreType.DMA((6,)),
            pltpu.SemaphoreType.DMA((9,)),
            pltpu.SemaphoreType.DMA((replicas,)),
            pltpu.SemaphoreType.DMA((8, 2)),
            pltpu.SemaphoreType.DMA((replicas, 2)),
            pltpu.SemaphoreType.DMA((replicas,)),
            pltpu.SemaphoreType.DMA((replicas,)),
            pltpu.SemaphoreType.DMA((9, 2)),
            pltpu.SemaphoreType.DMA((9, 2)),
            pltpu.SemaphoreType.DMA((2,)),
        ],
        compiler_params=pltpu.CompilerParams(
            collective_id=0, has_side_effects=True, vmem_limit_bytes=56 * 1024 * 1024
        ),
    )(
        activations.reshape(pixels, channels),
        preactivation.reshape(pixels, channels),
        upstream.reshape(pixels, channels),
        weights[0],
        master.reshape(flat),
        momentum.reshape(flat),
    )
    new_momentum = 0.9 * momentum + 0.0625 * combined
    new_weights = master - 0.02 * new_momentum
    return (
        passed.reshape(activations.shape),
        new_momentum.reshape(owned),
        new_weights.reshape(owned),
    )


def pick(sections, replicas, *arrays):
    activations, weights, momentum = arrays[0], arrays[3], arrays[5]
    channels = activations.shape[5]
    fits = (
        replicas == 8
        and activations.shape[2] == 1
        and weights.shape[1] == 9 * channels
        and weights.shape[2] == channels
        and channels == 3 * 128
        and (activations.shape[3] * activations.shape[4]) % 128 == 0
        and activations.shape[4] % 16 == 0
        and momentum.shape[2] % 1024 == 0
    )
    return factor_body(sections, replicas, *arrays) if fits else body(*arrays)


def solution(mesh):
    return jax.shard_map(
        functools.partial(pick, mesh.shape["pipe"], mesh.shape["rep"]),
        mesh=mesh,
        in_specs=(
            P("pipe", "rep", None, None, None, None),
            P("pipe", "rep", None, None, None, None),
            P("pipe", "rep", None, None, None, None),
            P("pipe", None, None),
            P("pipe", "rep", None),
            P("pipe", "rep", None),
        ),
        out_specs=(
            P("pipe", "rep", None, None, None, None),
            P("pipe", "rep", None),
            P("pipe", "rep", None),
        ),
        check_vma=False,
    )
```
